32 devices in a mesh: groups: 2 (over y), ctx: 16 (over z, x, core).
Axes of the slice: x: 2, y: 2, z: 4, core: 2. Of those that a mesh axis runs over, the one named last changes fastest.
Arguments:
- hidden: bfloat16 [4, 4, 8192], P(None, 'groups', 'ctx'), parts along dimension 1, may hold values from -6 to 6
- norm_gain: bfloat16 [8192], P('ctx'), may hold values from 0.5 to 1.5
- w_query: bfloat16 [8192, 8192], P('ctx')
- w_key: bfloat16 [8192, 1024], P('ctx'), may hold values from -0.25 to 0.25
- w_value: bfloat16 [8192, 1024], P('ctx'), may hold values from -0.125 to 0.125
- w_output: bfloat16 [8192, 8192], P('ctx'), may hold values from -0.09375 to 0.09375
- key_cache: bfloat16 [512, 128, 8, 128], P(('groups', 'ctx')), parts along dimension 0, may hold values from -6 to 6
- value_cache: bfloat16 [512, 128, 8, 128], P(('groups', 'ctx')), parts along dimension 0, may hold values from -6 to 6
- retrieval: int32 [8], replicated, may hold values from 0 to 1, as said below
- page_table: int32 [4, 128], P('groups'), parts along dimension 0, may hold values from 0 to 255, as said below
- lengths: int32 [4], P('groups'), parts along dimension 0, may hold values from 4096 to 16384, as said below
- window_start: int32 [4], P('groups'), parts along dimension 0, may hold values from 2945 to 15360, as said below
Outputs:
- attention_out: bfloat16 [4, 4, 8192], P(None, 'groups', 'ctx'), parts along dimension 1
The draws below stay inside these ranges and needn't reach their ends.
There are 2 independent parts, one for each index of `groups`. The reference program is written for one: setup_inputs(seed, part) draws one part's arguments, and reference() takes and returns one part's arrays. A program takes and returns all parts, laid end to end along the dimension named above; an argument that names none is the same for every part. Nothing has to cross between parts.
Inputs may be any that keep to these rules, and one draw needn't show every extreme that they name: `retrieval`: at least one key/value head of each kind. `page_table`: every page number appears exactly once; page g is row g of key_cache and value_cache. `lengths`: some request has exactly 16384 cached positions. lengths[b] - 1152 < window_start[b] <= lengths[b] - 1024.
All inputs are finite; a program needn't handle non-finite values.
Results may differ from the reference program's by a relative error of at most 0.0034.
The reference program's roundings to bfloat16 on the way (of `normed`, `query` and `attended`) count: a program that leaves them out, or rounds other values in their place, can miss the bound.
Values sent between devices are 32-bit elements; how exact they have to be, the bound alone decides.
A program may use at most 128 MiB of HBM per device.

```python
import math
import jax
import jax.numpy as jnp
from jax import lax

D = 8192
HEADS = 64
KV_HEADS = 8
HEAD_DIM = 128
STEPS = 4
BATCH = 2
PAGE = 128
WINDOW = 1024
SINKS = 4
PAGES_DEV = 16
BLOCKS = 128
CAP = 16384
N_CTX = 16


def request_bounds(key):
    base_key = jax.random.fold_in(key, 11)
    key_len, key_full, key_back = jax.random.split(base_key, 3)
    lowest = max(CAP // 4, WINDOW + 2 * PAGE)
    drawn = jax.random.randint(key_len, (BATCH,), lowest, CAP + 1)
    full_req = jax.random.randint(key_full, (), 0, BATCH)
    is_full = jnp.arange(BATCH) == full_req
    drawn = jnp.where(is_full, CAP, drawn)
    back_off = jax.random.randint(key_back, (BATCH,), 0, PAGE)
    back_off = jnp.where(is_full, 0, back_off)
    starts = drawn - WINDOW - back_off
    return (drawn.astype(jnp.int32), starts.astype(jnp.int32))


def draw_lengths(key, part):
    return request_bounds(key)[0]


def draw_window_start(key, part):
    return request_bounds(key)[1]


def draw_page_table(key, part):
    order = jax.random.permutation(jax.random.fold_in(key, 3), BATCH * BLOCKS)
    return order.reshape(BATCH, BLOCKS).astype(jnp.int32)


def draw_retrieval(key, part):
    key_count, key_perm = jax.random.split(jax.random.fold_in(key, 5), 2)
    count_full = jax.random.randint(key_count, (), 1, KV_HEADS)
    ranking = jax.random.permutation(key_perm, KV_HEADS)
    return (ranking < count_full).astype(jnp.int32)


def draw_w_query(key, part):
    key_noise, key_rank = jax.random.split(jax.random.fold_in(key, 7), 2)
    noise = jax.random.normal(key_noise, (D, HEADS * HEAD_DIM), jnp.float32)
    ranking = jax.random.permutation(key_rank, HEADS).astype(jnp.float32)
    strength = jnp.exp(ranking * (math.log(32.0) / (HEADS - 1)))
    column_scale = jnp.repeat(strength, HEAD_DIM)
    return (noise * column_scale[None, :] * D ** (-0.5)).astype(jnp.bfloat16)


def draw_key_cache(key, part):
    key_base, key_pick = jax.random.split(jax.random.fold_in(key, 13), 2)
    full_shape = (BATCH * BLOCKS, PAGE, KV_HEADS, HEAD_DIM)
    base = jnp.clip(jax.random.normal(key_base, full_shape, jnp.float32), -6.0, 6.0)
    rate = 16.0 / (BATCH * BLOCKS * PAGE)
    chosen = jax.random.uniform(key_pick, (BATCH * BLOCKS, PAGE, KV_HEADS, 1), jnp.float32) < rate
    strong = jnp.clip(5.0 * base, -6.0, 6.0)
    return jnp.where(chosen, strong, base).astype(jnp.bfloat16)


def with_spikes(values, stream_key, source, target, parts, factor):
    def block_of(position):
        return (jnp.arange(values.shape[position]) // (values.shape[position] // parts)).reshape((-1,) + (1,) * (values.ndim - 1 - position))

    near = jax.random.permutation(stream_key, parts)[block_of(target)]
    far = (block_of(target) + parts // 2) % parts
    return jnp.where((block_of(source) == near) | (block_of(source) == far), factor * values, values)


def shard_levels(rng, shape, pieces, low, top_value):
    level = 1.0
    for axis_at, parts in pieces:
        heights = jax.random.uniform(jax.random.fold_in(jax.random.fold_in(rng, 6), axis_at), (parts,), jnp.float32, low / len(pieces), top_value / len(pieces))
        level = level * jnp.repeat(jnp.exp(heights), shape[axis_at] // parts).reshape((-1,) + (1,) * (len(shape) - 1 - axis_at))
    return level


def normal_values(own_key, shape, scale, reach, pieces=(), held_as=jnp.bfloat16):
    factor_of = shard_levels(own_key, shape, pieces, -0.22, 0.18) if pieces else 1.0
    array = jax.random.normal(own_key, shape, jnp.float32) * scale * factor_of
    return jnp.minimum(jnp.maximum(array, -reach), reach).astype(held_as)


def bell_draw_with(rng, extent, spread, limit, shards, heavy, kind=jnp.bfloat16):
    array = spread * jax.random.normal(rng, extent, jnp.float32)
    if shards:
        array = array * shard_levels(rng, extent, shards, -0.22, 0.18)
    return jnp.clip(with_spikes(array, jax.random.fold_in(rng, 3), *heavy), -limit, limit).astype(kind)


def setup_inputs(seed: int = 0, part: int = 0) -> dict:
    streams_of = jax.random.split(jax.random.key(seed), 13)
    part_splits = jax.random.split(jax.random.fold_in(streams_of[12], part), 13)
    return {
        "hidden": normal_values(part_splits[0], (STEPS, BATCH, D), 1.0, 6.0, ((2, 16),)),
        "norm_gain": jnp.clip(1.0 + 0.1 * jax.random.normal(streams_of[1], (D,), jnp.float32), 0.5, 1.5).astype(jnp.bfloat16),
        "w_query": draw_w_query(jax.random.fold_in(streams_of[12], 71), part),
        "w_key": normal_values(streams_of[3], (D, KV_HEADS * HEAD_DIM), (D // 16) ** -0.5, 0.25, ((0, 16),)),
        "w_value": normal_values(streams_of[4], (D, KV_HEADS * HEAD_DIM), (D // 4) ** -0.5, 0.125, ((0, 16),)),
        "w_output": bell_draw_with(streams_of[5], (HEADS * HEAD_DIM, D), (HEADS * HEAD_DIM) ** -0.5, 0.09375, ((0, 16),), (0, 1, 16, 2.0)),
        "key_cache": draw_key_cache(jax.random.fold_in(jax.random.fold_in(streams_of[12], part), 71), part),
        "value_cache": normal_values(part_splits[7], (BATCH * BLOCKS, PAGE, KV_HEADS, HEAD_DIM), 1.0, 6.0, ((0, 16),)),
        "retrieval": draw_retrieval(jax.random.fold_in(streams_of[12], 71), part),
        "page_table": draw_page_table(jax.random.fold_in(jax.random.fold_in(streams_of[12], part), 71), part),
        "lengths": draw_lengths(jax.random.fold_in(jax.random.fold_in(streams_of[12], part), 71), part),
        "window_start": draw_window_start(jax.random.fold_in(jax.random.fold_in(streams_of[12], part), 71), part),
    }


very_low = -1e+30
epsilon = 1e-05

def combine(earlier, later):
    top_a, total_a, summed_a = earlier
    top_b, total_b, summed_b = later
    highest = jnp.maximum(top_a, top_b)
    factor_a = jnp.exp(top_a - highest)
    factor_b = jnp.exp(top_b - highest)
    return (highest, total_a * factor_a + total_b * factor_b, summed_a * factor_a[..., None] + summed_b * factor_b[..., None])

def arrange(top_val, total_val, summed_val, row_count):
    head_count = top_val.shape[1] * top_val.shape[2]
    top_val = jnp.transpose(top_val, (3, 0, 1, 2)).reshape(row_count, head_count)
    total_val = jnp.transpose(total_val, (3, 0, 1, 2)).reshape(row_count, head_count)
    summed_val = jnp.transpose(summed_val, (3, 0, 1, 2, 4)).reshape(row_count, head_count, summed_val.shape[-1])
    return (top_val, total_val, summed_val)

def page_partials(query_heads, page_keys, page_values, retrieval, page_table, lengths, window_start, first_page):
    page_count, page_len, kv_heads, head_dim = page_keys.shape
    batch_size, blocks = page_table.shape
    steps_n = query_heads.shape[0]
    slot_ids = first_page + jnp.arange(page_count, dtype=jnp.int32)
    matches = (page_table[None, :, :] == slot_ids[:, None, None]).astype(jnp.int32)
    owner_req = lax.optimization_barrier(jnp.sum(matches * jnp.arange(batch_size, dtype=jnp.int32)[None, :, None], axis=(1, 2)))
    block_ids = lax.optimization_barrier(jnp.sum(matches * jnp.arange(blocks, dtype=jnp.int32)[None, None, :], axis=(1, 2)))
    query_page = query_heads[:, owner_req].astype(jnp.float32)
    scores = jnp.einsum('spkgd,ptkd->pkgst', query_page, page_keys.astype(jnp.float32)) * head_dim ** (-0.5)
    positions = block_ids[:, None] * page_len + jnp.arange(page_len, dtype=jnp.int32)[None, :]
    in_range = positions < lengths[owner_req][:, None]
    recent = (positions < SINKS) | (positions >= window_start[owner_req][:, None])
    visible = in_range[:, None, :] & ((retrieval[None, :, None] == 1) | recent[:, None, :])
    visible = visible[:, :, None, None, :]
    masked = jnp.where(visible, scores, very_low)
    owner_hot = owner_req[:, None] == jnp.arange(batch_size, dtype=jnp.int32)[None, :]
    page_max = lax.optimization_barrier(jnp.max(masked, axis=-1))
    local_max = lax.optimization_barrier(jnp.max(jnp.where(owner_hot[:, :, None, None, None], page_max[:, None], very_low), axis=0))
    row_max = local_max[owner_req]
    weights = jnp.where(visible, jnp.exp(masked - row_max[..., None]), 0.0)
    owner_float = owner_hot.astype(jnp.float32)
    local_total = jnp.einsum('pb,pkgs->bkgs', owner_float, lax.optimization_barrier(jnp.sum(weights, axis=-1)), precision=lax.Precision.HIGHEST)
    rounded = weights.astype(jnp.bfloat16).astype(jnp.float32)
    values = jnp.einsum('pkgst,ptkd->pkgsd', rounded, page_values.astype(jnp.float32))
    local_sum = jnp.einsum('pb,pkgsd->bkgsd', owner_float, values, precision=lax.Precision.HIGHEST)
    return arrange(local_max, local_total, local_sum, steps_n * batch_size)

def fresh_partials(query_heads, key_heads, value_heads):
    steps_n, batch_size, kv_heads, group, head_dim = query_heads.shape
    scores = jnp.einsum('sbkgd,ubkd->bkgsu', query_heads.astype(jnp.float32), key_heads.astype(jnp.float32)) * head_dim ** (-0.5)
    causal = jnp.arange(steps_n)[:, None] >= jnp.arange(steps_n)[None, :]
    masked = jnp.where(causal, scores, very_low)
    highest = lax.optimization_barrier(jnp.max(masked, axis=-1))
    weights = jnp.where(causal, jnp.exp(masked - highest[..., None]), 0.0)
    totals = lax.optimization_barrier(jnp.sum(weights, axis=-1))
    rounded = weights.astype(jnp.bfloat16).astype(jnp.float32)
    summed = jnp.einsum('bkgsu,ubkd->bkgsd', rounded, value_heads.astype(jnp.float32))
    return arrange(highest, totals, summed, steps_n * batch_size)

def reference(hidden, norm_gain, w_query, w_key, w_value, w_output, key_cache, value_cache, retrieval, page_table, lengths, window_start):
    steps_n, batch_size, width_full = hidden.shape
    row_count = steps_n * batch_size
    floated = hidden.astype(jnp.float32)
    squares = lax.optimization_barrier(jnp.sum(floated * floated, axis=-1)).reshape(row_count, 1)
    inv_rms = lax.rsqrt(squares / D + epsilon)
    normed = (floated * norm_gain.astype(jnp.float32)).astype(jnp.bfloat16).reshape(row_count, width_full)
    query = (jnp.dot(normed, w_query, preferred_element_type=jnp.float32) * inv_rms).astype(jnp.bfloat16)
    new_key = (jnp.dot(normed, w_key, preferred_element_type=jnp.float32) * inv_rms).astype(jnp.bfloat16)
    new_value = (jnp.dot(normed, w_value, preferred_element_type=jnp.float32) * inv_rms).astype(jnp.bfloat16)
    query_heads = query.reshape(steps_n, batch_size, KV_HEADS, HEADS // KV_HEADS, HEAD_DIM)
    key_heads = new_key.reshape(steps_n, batch_size, KV_HEADS, HEAD_DIM)
    value_heads = new_value.reshape(steps_n, batch_size, KV_HEADS, HEAD_DIM)

    def visit_pages(running, group_index):
        first_page = (group_index * PAGES_DEV).astype(jnp.int32)
        page_keys = lax.dynamic_slice_in_dim(key_cache, first_page, PAGES_DEV, 0)
        page_values = lax.dynamic_slice_in_dim(value_cache, first_page, PAGES_DEV, 0)
        partial_value = page_partials(query_heads, page_keys, page_values, retrieval, page_table, lengths, window_start, first_page)
        return (combine(running, partial_value), None)
    start_state = (jnp.full((row_count, HEADS), very_low, jnp.float32), jnp.zeros((row_count, HEADS), jnp.float32), jnp.zeros((row_count, HEADS, HEAD_DIM), jnp.float32))
    running, _ = lax.scan(visit_pages, start_state, jnp.arange(N_CTX, dtype=jnp.int32))
    fresh_parts = fresh_partials(query_heads, key_heads, value_heads)
    highest, totals, summed = combine(running, fresh_parts)
    attended = (summed / totals[..., None]).reshape(row_count, HEADS * HEAD_DIM).astype(jnp.bfloat16)
    projected = jnp.dot(attended, w_output, preferred_element_type=jnp.float32).astype(jnp.bfloat16)
    return projected.reshape(steps_n, batch_size, width_full)
```

```python
import functools

import jax
import jax.numpy as jnp
from jax import lax
from jax.experimental import pallas as pl
from jax.experimental.pallas import tpu as pltpu
from jax.sharding import PartitionSpec as P

D = 8192
SINKS = 4


very_low = -1e30
epsilon = 1e-05


def merged_2(shard, axis, combine):
    everything = jax.tree.map(lambda part: lax.all_gather(part, axis), shard)
    first = jax.tree.map(lambda part: part[0], everything)

    def turn(k, so_far):
        return combine(so_far, jax.tree.map(lambda part: part[k], everything))

    return lax.fori_loop(1, lax.axis_size(axis), turn, first)


def combine(earlier, later):
    top_a, total_a, summed_a = earlier
    top_b, total_b, summed_b = later
    highest = jnp.maximum(top_a, top_b)
    factor_a = jnp.exp(top_a - highest)
    factor_b = jnp.exp(top_b - highest)
    return (
        highest,
        total_a * factor_a + total_b * factor_b,
        summed_a * factor_a[..., None] + summed_b * factor_b[..., None],
    )


def arrange(top_val, total_val, summed_val, row_count):
    head_count = top_val.shape[1] * top_val.shape[2]
    top_val = jnp.transpose(top_val, (3, 0, 1, 2)).reshape(row_count, head_count)
    total_val = jnp.transpose(total_val, (3, 0, 1, 2)).reshape(row_count, head_count)
    summed_val = jnp.transpose(summed_val, (3, 0, 1, 2, 4)).reshape(
        row_count, head_count, summed_val.shape[-1]
    )
    return (top_val, total_val, summed_val)


def of_owner(values, owner_req, axis):
    picked = None
    for b in range(values.shape[axis]):
        entry = lax.slice_in_dim(values, b, b + 1, axis=axis)
        mine = (owner_req == b).reshape((-1,) + (1,) * (values.ndim - 1 - axis))
        picked = entry if picked is None else jnp.where(mine, entry, picked)
    shape = list(values.shape)
    shape[axis] = owner_req.shape[0]
    return jnp.broadcast_to(picked, shape)


def page_partials(
    query_heads, page_keys, page_values, retrieval, page_table, lengths, window_start, first_page
):
    page_count, page_len, kv_heads, head_dim = page_keys.shape
    batch_size, blocks = page_table.shape
    steps_n = query_heads.shape[0]
    slot_ids = first_page + jnp.arange(page_count, dtype=jnp.int32)
    matches = (page_table[None, :, :] == slot_ids[:, None, None]).astype(jnp.int32)
    owner_req = jnp.sum(
        matches * jnp.arange(batch_size, dtype=jnp.int32)[None, :, None], axis=(1, 2)
    )
    block_ids = jnp.sum(matches * jnp.arange(blocks, dtype=jnp.int32)[None, None, :], axis=(1, 2))
    query_page = of_owner(query_heads, owner_req, 1)
    scores = jnp.einsum(
        "spkgd,ptkd->pkgst", query_page, page_keys, preferred_element_type=jnp.float32
    ) * head_dim ** (-0.5)
    positions = block_ids[:, None] * page_len + jnp.arange(page_len, dtype=jnp.int32)[None, :]
    in_range = positions < of_owner(lengths, owner_req, 0)[:, None]
    recent = (positions < SINKS) | (positions >= of_owner(window_start, owner_req, 0)[:, None])
    visible = in_range[:, None, :] & ((retrieval[None, :, None] == 1) | recent[:, None, :])
    visible = visible[:, :, None, None, :]
    masked = jnp.where(visible, scores, very_low)
    owner_hot = owner_req[:, None] == jnp.arange(batch_size, dtype=jnp.int32)[None, :]
    page_max = jnp.max(masked, axis=-1)
    local_max = jnp.max(
        jnp.where(owner_hot[:, :, None, None, None], page_max[:, None], very_low), axis=0
    )
    row_max = of_owner(local_max, owner_req, 0)
    weights = jnp.where(visible, jnp.exp(masked - row_max[..., None]), 0.0)
    owner_float = owner_hot.astype(jnp.float32)
    local_total = jnp.einsum(
        "pb,pkgs->bkgs", owner_float, jnp.sum(weights, axis=-1), precision=lax.Precision.HIGHEST
    )
    values = jnp.einsum(
        "pkgst,ptkd->pkgsd",
        weights.astype(jnp.bfloat16),
        page_values,
        preferred_element_type=jnp.float32,
    )
    local_sum = jnp.einsum("pb,pkgsd->bkgsd", owner_float, values, precision=lax.Precision.HIGHEST)
    return arrange(local_max, local_total, local_sum, steps_n * batch_size)


def fresh_partials(query_heads, key_heads, value_heads):
    steps_n, batch_size, kv_heads, group, head_dim = query_heads.shape
    scores = jnp.einsum(
        "sbkgd,ubkd->bkgsu", query_heads, key_heads, preferred_element_type=jnp.float32
    ) * head_dim ** (-0.5)
    causal = jnp.arange(steps_n)[:, None] >= jnp.arange(steps_n)[None, :]
    masked = jnp.where(causal, scores, very_low)
    highest = jnp.max(masked, axis=-1)
    weights = jnp.where(causal, jnp.exp(masked - highest[..., None]), 0.0)
    totals = jnp.sum(weights, axis=-1)
    summed = jnp.einsum(
        "bkgsu,ubkd->bkgsd",
        weights.astype(jnp.bfloat16),
        value_heads,
        preferred_element_type=jnp.float32,
    )
    return arrange(highest, totals, summed, steps_n * batch_size)


def local_small(
    hidden,
    norm_gain,
    w_query,
    w_key,
    w_value,
    w_output,
    key_cache,
    value_cache,
    retrieval,
    page_table,
    lengths,
    window_start,
):
    steps_n, batch_size, width_local = hidden.shape
    row_count = steps_n * batch_size
    page_count, page_len, kv_heads, head_dim = key_cache.shape
    query_width = w_query.shape[1]
    head_count = query_width // head_dim
    floated = hidden.astype(jnp.float32)
    squares = jnp.sum(floated * floated, axis=-1).reshape(row_count, 1)
    normed = (
        (floated * norm_gain.astype(jnp.float32))
        .astype(jnp.bfloat16)
        .reshape(row_count, width_local)
    )
    query_part = jnp.dot(normed, w_query, preferred_element_type=jnp.float32)
    key_part = jnp.dot(normed, w_key, preferred_element_type=jnp.float32)
    value_part = jnp.dot(normed, w_value, preferred_element_type=jnp.float32)
    query_sum, key_sum, value_sum, square_sum = lax.psum(
        (query_part, key_part, value_part, squares), "ctx"
    )
    inv_rms = lax.rsqrt(square_sum / D + epsilon)
    query_heads = (
        (query_sum * inv_rms)
        .astype(jnp.bfloat16)
        .reshape(steps_n, batch_size, kv_heads, head_count // kv_heads, head_dim)
    )
    key_heads = (
        (key_sum * inv_rms).astype(jnp.bfloat16).reshape(steps_n, batch_size, kv_heads, head_dim)
    )
    value_heads = (
        (value_sum * inv_rms).astype(jnp.bfloat16).reshape(steps_n, batch_size, kv_heads, head_dim)
    )
    device = lax.axis_index("ctx")
    local_parts = page_partials(
        query_heads,
        key_cache,
        value_cache,
        retrieval,
        page_table,
        lengths,
        window_start,
        device * page_count,
    )
    fresh_parts = fresh_partials(query_heads, key_heads, value_heads)
    col_share = query_width // lax.axis_size("ctx")
    col_start = device * col_share
    merged = merged_2(local_parts, "ctx", combine)
    highest, totals, summed = combine(merged, fresh_parts)
    attended_full = (
        (summed / totals[..., None]).reshape(row_count, query_width).astype(jnp.bfloat16)
    )
    attended = lax.dynamic_slice_in_dim(attended_full, col_start, col_share, 1)
    partial_out = jnp.dot(attended, w_output, preferred_element_type=jnp.float32)
    reduced = lax.psum_scatter(partial_out, "ctx", scatter_dimension=1, tiled=True)
    return reduced.reshape(steps_n, batch_size, -1).astype(jnp.bfloat16)


log2_e = 1.4426950408889634
chips = 8
far_away = 2**30


def fused(
    n,
    steps_n,
    batch,
    page_len,
    retrieval_ref,
    lengths_ref,
    window_ref,
    hidden_ref,
    gain_ref,
    table_ref,
    wq_hbm,
    wk_hbm,
    wv_hbm,
    wo_hbm,
    keys_hbm,
    values_hbm,
    out_ref,
    wq_v,
    wkv_v,
    wo_v,
    keys_v,
    values_v,
    keys_t,
    values_k,
    apart,
    bias,
    msg1,
    twin1,
    recv1,
    fresh_kv,
    gath,
    part3,
    twin3,
    msg3,
    recv3,
    out_own,
    out_other,
    twin4,
    recv4,
    load_sem,
    send_sem,
    recv_sem,
):
    f32, bf16 = jnp.float32, jnp.bfloat16
    me = lax.axis_index("ctx")
    chip, core = me // 2, lax.rem(me, 2)
    other = 1 - core
    pages = keys_v.shape[0]
    dim = 128
    rows = steps_n * batch
    heads_own = 4
    q_rows = heads_own * rows
    share = heads_own * dim
    width_local = hidden_ref.shape[2]
    scale = dim ** (-0.5) * log2_e

    def chip_at(i):
        where = 0
        for bit in (1, 2, 4):
            a, b = lax.rem(chip // bit, 2), (i // bit) % 2
            where = where + bit * (a + b - 2 * a * b)
        return where

    def peer(i):
        return 2 * chip_at(i) + core

    twin = 2 * chip + other

    def load(k, from_ref, to_ref):
        return pltpu.make_async_copy(from_ref, to_ref, load_sem.at[k])

    def remote(phase, i, from_ref, to_ref, device):
        return pltpu.make_async_remote_copy(
            src_ref=from_ref,
            dst_ref=to_ref,
            send_sem=send_sem.at[phase, i],
            recv_sem=recv_sem.at[phase, i],
            device_id={"ctx": device},
            device_id_type=pl.DeviceIdType.MESH,
        )

    kv_width = wk_hbm.shape[1]
    quarter = wq_hbm.shape[1] // 4
    some = pages // 4
    load_kv = [
        load(0, wk_hbm, wkv_v.at[:, pl.ds(0, kv_width)]),
        load(1, wv_hbm, wkv_v.at[:, pl.ds(kv_width, kv_width)]),
    ]
    columns = [pl.ds(j * quarter, quarter) for j in range(4)]
    load_wq = [load(2 + j, wq_hbm.at[:, c], wq_v.at[:, c]) for j, c in enumerate(columns)]
    load_wo = [load(6 + j, wo_hbm.at[:, c], wo_v.at[:, c]) for j, c in enumerate(columns)]
    page_sets = [pl.ds(j * some, some) for j in range(4)]
    load_keys = [load(10 + j, keys_hbm.at[c], keys_v.at[c]) for j, c in enumerate(page_sets)]
    load_values = [load(14 + j, values_hbm.at[c], values_v.at[c]) for j, c in enumerate(page_sets)]

    barrier = pltpu.get_barrier_semaphore()

    def greet(device):
        pl.semaphore_signal(
            barrier, inc=1, device_id={"ctx": device}, device_id_type=pl.DeviceIdType.MESH
        )

    @pl.loop(1, chips)
    def _(i):
        greet(peer(i))

    greet(twin)

    for copy in load_kv + load_wq + load_keys + load_values + load_wo:
        copy.start()

    loaded = hidden_ref[...].astype(f32)
    floated = jnp.concatenate(
        [loaded[s, b : b + 1, :] for b in range(batch) for s in range(steps_n)], axis=0
    )
    squares = jnp.sum(floated * floated, axis=1, keepdims=True)
    squares = jnp.broadcast_to(squares, (rows, dim))
    normed = (floated * gain_ref[...].astype(f32).reshape(1, width_local)).astype(bf16)

    sub = lax.broadcasted_iota(jnp.int32, (rows, dim), 0)
    lane = lax.broadcasted_iota(jnp.int32, (rows, dim), 1)
    first = sub < steps_n
    table = table_ref[...]
    page_id = lax.broadcasted_iota(jnp.int32, (pages, table.shape[1]), 0) + me * pages
    block = lax.broadcasted_iota(jnp.int32, (pages, table.shape[1]), 1).astype(f32)
    starts = []
    for b in range(batch):
        hit = jnp.where(table[b : b + 1, :] == page_id, 1.0, 0.0)
        found = jnp.sum(hit, axis=1, keepdims=True)
        start = jnp.sum(hit * block, axis=1, keepdims=True) * float(page_len)
        start = jnp.where(found > 0.0, start, float(far_away))
        starts.append(jnp.broadcast_to(start, (pages, dim)).astype(jnp.int32))
    until = jnp.where(first, lengths_ref[0], lengths_ref[1])
    since = jnp.where(first, window_ref[0], window_ref[1])
    for p in range(pages):
        position = jnp.where(first, starts[0][p : p + 1, :], starts[1][p : p + 1, :]) + lane
        cached = position < until
        recent = cached & ((position < SINKS) | (position >= since))
        bias[0, :, pl.ds(p * dim, dim)] = jnp.where(recent, 0.0, very_low)
        bias[1, :, pl.ds(p * dim, dim)] = jnp.where(cached, 0.0, very_low)

    for copy in load_kv:
        copy.wait()
    fresh = jnp.dot(normed, wkv_v[...], preferred_element_type=f32)
    for j in range(chips):
        slot = chip_at(j)
        for c in range(2):
            at = c * kv_width + j * dim
            msg1[c, slot, pl.ds(q_rows, rows), :] = fresh[:, at : at + dim]
            msg1[c, slot, pl.ds(q_rows + rows, rows), :] = squares
    for j in range(chips):
        if j % 4 == 0:
            load_wq[j // 2].wait()
            load_wq[j // 2 + 1].wait()
        slot = chip_at(j)
        query = jnp.dot(
            normed, wq_v[:, pl.ds(j * 2 * share, 2 * share)], preferred_element_type=f32
        )
        for c in range(2):
            for g in range(heads_own):
                at = c * share + g * dim
                msg1[c, slot, pl.ds(g * rows, rows), :] = query[:, at : at + dim]

    pl.semaphore_wait(barrier, chips)

    remote(0, 0, msg1.at[other], twin1, twin).start()
    remote(0, 0, msg1.at[other], twin1, twin).wait_recv()

    @pl.loop(1, chips)
    def _(i):
        msg1[core, i] = msg1[core, i] + twin1[i]
        remote(0, i, msg1.at[core, i], recv1.at[i], peer(i)).start()

    def by_head(p, slot, from_ref):
        apart[slot] = from_ref[p].astype(f32)
        return [apart[slot, pl.ds(k, page_len, stride=chips), :] for k in range(chips)]

    def turn_keys(p, slot):
        at = pl.ds(pl.multiple_of(p * page_len, page_len), page_len)
        for k, part in enumerate(by_head(p, slot, keys_v)):
            keys_t[k, :, at] = part.T.astype(bf16)

    def sort_values(p, slot):
        at = pl.ds(pl.multiple_of(p * page_len, page_len), page_len)
        for k, part in enumerate(by_head(p, slot, values_v)):
            values_k[k, at, :] = part.astype(bf16)

    for copy in load_keys:
        copy.wait()

    @pl.loop(0, pages // 2)
    def _(h):
        for u in range(2):
            turn_keys(2 * h + u, u)

    for copy in load_values:
        copy.wait()

    values_early = pages // 4

    @pl.loop(0, values_early)
    def _(h):
        for u in range(2):
            sort_values(2 * h + u, u)

    def add_far(i, acc):
        remote(0, i, msg1.at[core, i], recv1.at[i], peer(i)).wait_recv()
        return acc + recv1[i]

    summed = lax.fori_loop(1, chips, add_far, msg1[core, 0] + twin1[0])
    inv_rms = lax.rsqrt(summed[q_rows + rows :] / (width_local * n) + epsilon)
    fresh_kv[core] = (summed[q_rows : q_rows + rows] * inv_rms).astype(bf16).astype(f32)
    for g in range(heads_own):
        piece = summed[g * rows : (g + 1) * rows] * inv_rms
        gath[0, core, pl.ds(g * rows, rows), :] = piece.astype(bf16).astype(f32)

    own = gath.at[0, core]

    @pl.loop(1, chips)
    def _(i):
        remote(1, i, own, gath.at[i, core], peer(i)).start()

    remote(2, 0, own, own, twin).start()
    remote(3, 0, fresh_kv.at[core], fresh_kv.at[core], twin).start()

    @pl.loop(values_early, pages // 2)
    def _(h):
        for u in range(2):
            sort_values(2 * h + u, u)

    @pl.loop(1, chips)
    def _(i):
        block = gath.at[i, core]
        remote(1, i, own, block, peer(i)).wait_recv()
        remote(2, i, block, block, twin).start()

    def scores_of(i):
        k = chip_at(i)
        query = gath[i].reshape(2 * q_rows, dim).astype(bf16)
        scores = jnp.dot(query, keys_t[k], preferred_element_type=f32)
        hidden_by = bias[retrieval_ref[k]]
        scores = scores.reshape(2 * heads_own, rows, pages * page_len) * scale + hidden_by[None]
        return scores.reshape(2 * q_rows, pages * page_len)

    def fold(op, wide):
        parts = [wide[:, p * dim : (p + 1) * dim] for p in range(pages)]
        while len(parts) > 1:
            parts = [op(a, b) for a, b in zip(parts[::2], parts[1::2])]
        return parts[0]

    def weigh(scores):
        highest = jnp.max(fold(jnp.maximum, scores), axis=1, keepdims=True)
        weights = jnp.exp2(scores - highest)
        total = jnp.sum(fold(jnp.add, weights), axis=1, keepdims=True)
        return highest, total, weights.astype(bf16)

    def attend(offsets):
        scored = [scores_of(i) for i in offsets]
        weighed = [weigh(scores) for scores in scored]
        for i, (highest, total, weights) in zip(offsets, weighed):
            summed = jnp.dot(weights, values_k[chip_at(i)], preferred_element_type=f32)
            highest = jnp.broadcast_to(highest, summed.shape)
            total = jnp.broadcast_to(total, summed.shape)
            for c in range(2):
                mine = slice(c * q_rows, (c + 1) * q_rows)
                part3[i, c, pl.ds(0, q_rows), :] = summed[mine]
                part3[i, c, pl.ds(q_rows, q_rows), :] = highest[mine]
                part3[i, c, pl.ds(2 * q_rows, q_rows), :] = total[mine]
            remote(3, 1 + i, part3.at[i, other], twin3.at[i], twin).start()

    row = lax.broadcasted_iota(jnp.int32, (q_rows, dim), 0)
    col = lax.broadcasted_iota(jnp.int32, (q_rows, dim), 1)

    def join(i):
        remote(3, 1 + i, part3.at[i, other], twin3.at[i], twin).wait_recv()
        a, b = part3[i, core], twin3[i]
        top_a, top_b = a[q_rows : 2 * q_rows], b[q_rows : 2 * q_rows]
        top = jnp.maximum(top_a, top_b)
        factor_a, factor_b = jnp.exp2(top_a - top), jnp.exp2(top_b - top)
        summed = a[:q_rows] * factor_a + b[:q_rows] * factor_b
        total = a[2 * q_rows :] * factor_a + b[2 * q_rows :] * factor_b
        stats = jnp.where(col == row, top, 0.0) + jnp.where(col == row + q_rows, total, 0.0)
        stats = jnp.sum(stats, axis=0, keepdims=True)
        return summed, jnp.broadcast_to(stats, (rows, dim))

    def pass_on(i):
        summed, stats = join(i)
        msg3[i, pl.ds(0, q_rows), :] = summed
        msg3[i, pl.ds(q_rows, rows), :] = stats
        remote(4, i, msg3.at[i], recv3.at[i], peer(i)).start()

    def arrived(i):
        origin = gath.at[i, other]
        remote(2, i, origin, origin, twin).wait_recv()

    arrived(0)
    remote(3, 0, fresh_kv.at[other], fresh_kv.at[other], twin).wait_recv()
    arrived(1)
    attend([0, 1])
    summed, stats = join(0)
    recv3[0, pl.ds(0, q_rows), :] = summed
    recv3[0, pl.ds(q_rows, rows), :] = stats

    @pl.loop(1, chips // 2)
    def _(h):
        arrived(2 * h)
        arrived(2 * h + 1)
        attend([2 * h, 2 * h + 1])

        @pl.when(h > 1)
        def _():
            pass_on(2 * h - 2)

        pass_on(2 * h - 1)

    pass_on(chips - 2)
    pass_on(chips - 1)

    new_key = jnp.concatenate([fresh_kv[0]] * (dim // rows), axis=0).astype(bf16)
    new_value = jnp.concatenate([fresh_kv[1]] * (dim // rows), axis=0).astype(bf16)
    scores = lax.dot_general(
        gath[0, core].astype(bf16), new_key, (((1,), (1,)), ((), ())), preferred_element_type=f32
    )
    token = lax.rem(row, rows)
    causal = (col < rows) & (col // steps_n == token // steps_n) & (col <= token)
    scores = jnp.where(causal, scores * scale, very_low)
    fresh_top = jnp.max(scores, axis=1, keepdims=True)
    weights = jnp.where(causal, jnp.exp2(scores - fresh_top), 0.0)
    fresh_total = jnp.sum(weights, axis=1, keepdims=True)
    fresh_sum = jnp.dot(weights.astype(bf16), new_value, preferred_element_type=f32)

    for copy in load_wo:
        copy.wait()

    @pl.loop(1, chips)
    def _(i):
        remote(4, i, msg3.at[i], recv3.at[i], peer(i)).wait_recv()

    stats = jnp.zeros((rows, dim), f32)
    for i in range(chips):
        stats = jnp.where(sub == i, recv3[i, pl.ds(q_rows, rows), :], stats)
    stats = jnp.concatenate([stats] * (dim // rows), axis=0).T
    top = jnp.where(col < chips, stats[:q_rows], jnp.where(col == chips, fresh_top, very_low))
    total = jnp.where(
        col < chips, stats[q_rows : 2 * q_rows], jnp.where(col == chips, fresh_total, 0.0)
    )
    factor = jnp.exp2(top - jnp.max(top, axis=1, keepdims=True))
    factor = factor / jnp.sum(factor * total, axis=1, keepdims=True)
    acc = fresh_sum * factor[:, chips : chips + 1]
    for i in range(chips):
        acc += recv3[i, pl.ds(0, q_rows), :] * factor[:, i : i + 1]
    attended = jnp.concatenate(
        [acc[g * rows : (g + 1) * rows] for g in range(heads_own)], axis=1
    ).astype(bf16)

    def project_out(j, c):
        at = pl.multiple_of(j * 2 * share + c * share, share)
        return jnp.dot(attended, wo_v[:, pl.ds(at, share)], preferred_element_type=f32)

    for j in range(chips):
        out_other[chip_at(j)] = project_out(j, other)
    remote(5, 0, out_other, twin4, twin).start()
    for j in range(chips):
        out_own[chip_at(j)] = project_out(j, core)
    remote(5, 0, out_other, twin4, twin).wait_recv()

    @pl.loop(1, chips)
    def _(i):
        out_own[i] = out_own[i] + twin4[i]
        remote(5, i, out_own.at[i], recv4.at[i], peer(i)).start()

    def add_out(i, acc):
        remote(5, i, out_own.at[i], recv4.at[i], peer(i)).wait_recv()
        return acc + recv4[i]

    result = lax.fori_loop(1, chips, add_out, out_own[0] + twin4[0])
    for s in range(steps_n):
        out_ref[s] = jnp.concatenate(
            [result[b * steps_n + s : b * steps_n + s + 1] for b in range(batch)], axis=0
        ).astype(out_ref.dtype)

    remote(0, 0, msg1.at[other], twin1, twin).wait_send()
    remote(2, 0, own, own, twin).wait_send()
    remote(3, 0, fresh_kv.at[core], fresh_kv.at[core], twin).wait_send()
    remote(3, 1, part3.at[0, other], twin3.at[0], twin).wait_send()
    remote(5, 0, out_other, twin4, twin).wait_send()

    @pl.loop(1, chips)
    def _(i):
        remote(0, i, msg1.at[core, i], recv1.at[i], peer(i)).wait_send()
        remote(1, i, own, gath.at[i, core], peer(i)).wait_send()
        remote(2, i, gath.at[i, core], gath.at[i, core], twin).wait_send()
        remote(3, 1 + i, part3.at[i, other], twin3.at[i], twin).wait_send()
        remote(4, i, msg3.at[i], recv3.at[i], peer(i)).wait_send()
        remote(5, i, out_own.at[i], recv4.at[i], peer(i)).wait_send()


def local(
    hidden,
    norm_gain,
    w_query,
    w_key,
    w_value,
    w_output,
    key_cache,
    value_cache,
    retrieval,
    page_table,
    lengths,
    window_start,
):
    n = lax.axis_size("ctx")
    steps_n, batch, width_local = hidden.shape
    pages, page_len, kv_heads, dim = key_cache.shape
    query_width = w_query.shape[1]
    share = query_width // n
    rows = steps_n * batch
    q_rows = query_width // dim * steps_n
    if pages % 4 or (n, share, rows, batch, kv_heads, dim, page_len) != (16, 512, 8, 2, 8, 128, 128):
        return local_small(
            hidden,
            norm_gain,
            w_query,
            w_key,
            w_value,
            w_output,
            key_cache,
            value_cache,
            retrieval,
            page_table,
            lengths,
            window_start,
        )
    f32, bf16 = jnp.float32, jnp.bfloat16
    smem = pl.BlockSpec(memory_space=pltpu.SMEM)
    vmem = pl.BlockSpec(memory_space=pltpu.VMEM)
    hbm = pl.BlockSpec(memory_space=pl.ANY)
    dma = pltpu.SemaphoreType.DMA
    positions = pages * page_len
    out = pl.pallas_call(
        functools.partial(fused, n, steps_n, batch, page_len),
        out_shape=jax.ShapeDtypeStruct((steps_n, batch, w_output.shape[1] // n), bf16),
        in_specs=[smem] * 3 + [vmem] * 3 + [hbm] * 6,
        out_specs=vmem,
        scratch_shapes=[
            pltpu.VMEM((width_local, query_width), bf16),
            pltpu.VMEM((width_local, 2 * kv_heads * dim), bf16),
            pltpu.VMEM((share, w_output.shape[1]), bf16),
            pltpu.VMEM((pages, page_len * kv_heads, dim), bf16),
            pltpu.VMEM((pages, page_len * kv_heads, dim), bf16),
            pltpu.VMEM((kv_heads, dim, positions), bf16),
            pltpu.VMEM((kv_heads, positions, dim), bf16),
            pltpu.VMEM((2, page_len * kv_heads, dim), f32),
            pltpu.VMEM((2, rows, positions), f32),
            pltpu.VMEM((2, chips, 48, dim), f32),
            pltpu.VMEM((chips, 48, dim), f32),
            pltpu.VMEM((chips, 48, dim), f32),
            pltpu.VMEM((2, rows, dim), f32),
            pltpu.VMEM((chips, 2, 32, dim), f32),
            pltpu.VMEM((chips, 2, 96, dim), f32),
            pltpu.VMEM((chips, 96, dim), f32),
            pltpu.VMEM((chips, 40, dim), f32),
            pltpu.VMEM((chips, 40, dim), f32),
            pltpu.VMEM((chips, rows, share), f32),
            pltpu.VMEM((chips, rows, share), f32),
            pltpu.VMEM((chips, rows, share), f32),
            pltpu.VMEM((chips, rows, share), f32),
            dma((18,)),
            dma((6, chips + 1)),
            dma((6, chips + 1)),
        ],
        compiler_params=pltpu.CompilerParams(
            collective_id=0, has_side_effects=True, vmem_limit_bytes=56 * 2**20
        ),
    )(
        retrieval,
        lengths,
        window_start,
        hidden,
        norm_gain,
        page_table,
        w_query,
        w_key,
        w_value,
        w_output,
        key_cache.reshape(pages, page_len * kv_heads, dim),
        value_cache.reshape(pages, page_len * kv_heads, dim),
    )
    return out


def solution(mesh):
    placed = (
        P(None, "groups", "ctx"),
        P("ctx"),
        P("ctx", None),
        P("ctx", None),
        P("ctx", None),
        P("ctx", None),
        P(("groups", "ctx"), None, None, None),
        P(("groups", "ctx"), None, None, None),
        P(),
        P("groups", None),
        P("groups"),
        P("groups"),
    )
    return jax.shard_map(
        local, mesh=mesh, in_specs=placed, out_specs=P(None, "groups", "ctx"), check_vma=False
    )
```

```python
import functools

import jax
import jax.numpy as jnp
from jax import lax
from jax.experimental import pallas as pl
from jax.experimental.pallas import tpu as pltpu
from jax.sharding import PartitionSpec as P

D = 8192
SINKS = 4


very_low = -1e30
epsilon = 1e-05


def merged_2(shard, axis, combine):
    everything = jax.tree.map(lambda part: lax.all_gather(part, axis), shard)
    first = jax.tree.map(lambda part: part[0], everything)

    def turn(k, so_far):
        return combine(so_far, jax.tree.map(lambda part: part[k], everything))

    return lax.fori_loop(1, lax.axis_size(axis), turn, first)


def combine(earlier, later):
    top_a, total_a, summed_a = earlier
    top_b, total_b, summed_b = later
    highest = jnp.maximum(top_a, top_b)
    factor_a = jnp.exp(top_a - highest)
    factor_b = jnp.exp(top_b - highest)
    return (
        highest,
        total_a * factor_a + total_b * factor_b,
        summed_a * factor_a[..., None] + summed_b * factor_b[..., None],
    )


def arrange(top_val, total_val, summed_val, row_count):
    head_count = top_val.shape[1] * top_val.shape[2]
    top_val = jnp.transpose(top_val, (3, 0, 1, 2)).reshape(row_count, head_count)
    total_val = jnp.transpose(total_val, (3, 0, 1, 2)).reshape(row_count, head_count)
    summed_val = jnp.transpose(summed_val, (3, 0, 1, 2, 4)).reshape(
        row_count, head_count, summed_val.shape[-1]
    )
    return (top_val, total_val, summed_val)


def of_owner(values, owner_req, axis):
    picked = None
    for b in range(values.shape[axis]):
        entry = lax.slice_in_dim(values, b, b + 1, axis=axis)
        mine = (owner_req == b).reshape((-1,) + (1,) * (values.ndim - 1 - axis))
        picked = entry if picked is None else jnp.where(mine, entry, picked)
    shape = list(values.shape)
    shape[axis] = owner_req.shape[0]
    return jnp.broadcast_to(picked, shape)


def page_partials(
    query_heads, page_keys, page_values, retrieval, page_table, lengths, window_start, first_page
):
    page_count, page_len, kv_heads, head_dim = page_keys.shape
    batch_size, blocks = page_table.shape
    steps_n = query_heads.shape[0]
    slot_ids = first_page + jnp.arange(page_count, dtype=jnp.int32)
    matches = (page_table[None, :, :] == slot_ids[:, None, None]).astype(jnp.int32)
    owner_req = jnp.sum(
        matches * jnp.arange(batch_size, dtype=jnp.int32)[None, :, None], axis=(1, 2)
    )
    block_ids = jnp.sum(matches * jnp.arange(blocks, dtype=jnp.int32)[None, None, :], axis=(1, 2))
    query_page = of_owner(query_heads, owner_req, 1)
    scores = jnp.einsum(
        "spkgd,ptkd->pkgst", query_page, page_keys, preferred_element_type=jnp.float32
    ) * head_dim ** (-0.5)
    positions = block_ids[:, None] * page_len + jnp.arange(page_len, dtype=jnp.int32)[None, :]
    in_range = positions < of_owner(lengths, owner_req, 0)[:, None]
    recent = (positions < SINKS) | (positions >= of_owner(window_start, owner_req, 0)[:, None])
    visible = in_range[:, None, :] & ((retrieval[None, :, None] == 1) | recent[:, None, :])
    visible = visible[:, :, None, None, :]
    masked = jnp.where(visible, scores, very_low)
    owner_hot = owner_req[:, None] == jnp.arange(batch_size, dtype=jnp.int32)[None, :]
    page_max = jnp.max(masked, axis=-1)
    local_max = jnp.max(
        jnp.where(owner_hot[:, :, None, None, None], page_max[:, None], very_low), axis=0
    )
    row_max = of_owner(local_max, owner_req, 0)
    weights = jnp.where(visible, jnp.exp(masked - row_max[..., None]), 0.0)
    owner_float = owner_hot.astype(jnp.float32)
    local_total = jnp.einsum(
        "pb,pkgs->bkgs", owner_float, jnp.sum(weights, axis=-1), precision=lax.Precision.HIGHEST
    )
    values = jnp.einsum(
        "pkgst,ptkd->pkgsd",
        weights.astype(jnp.bfloat16),
        page_values,
        preferred_element_type=jnp.float32,
    )
    local_sum = jnp.einsum("pb,pkgsd->bkgsd", owner_float, values, precision=lax.Precision.HIGHEST)
    return arrange(local_max, local_total, local_sum, steps_n * batch_size)


def fresh_partials(query_heads, key_heads, value_heads):
    steps_n, batch_size, kv_heads, group, head_dim = query_heads.shape
    scores = jnp.einsum(
        "sbkgd,ubkd->bkgsu", query_heads, key_heads, preferred_element_type=jnp.float32
    ) * head_dim ** (-0.5)
    causal = jnp.arange(steps_n)[:, None] >= jnp.arange(steps_n)[None, :]
    masked = jnp.where(causal, scores, very_low)
    highest = jnp.max(masked, axis=-1)
    weights = jnp.where(causal, jnp.exp(masked - highest[..., None]), 0.0)
    totals = jnp.sum(weights, axis=-1)
    summed = jnp.einsum(
        "bkgsu,ubkd->bkgsd",
        weights.astype(jnp.bfloat16),
        value_heads,
        preferred_element_type=jnp.float32,
    )
    return arrange(highest, totals, summed, steps_n * batch_size)


def local_small(
    hidden,
    norm_gain,
    w_query,
    w_key,
    w_value,
    w_output,
    key_cache,
    value_cache,
    retrieval,
    page_table,
    lengths,
    window_start,
):
    steps_n, batch_size, width_local = hidden.shape
    row_count = steps_n * batch_size
    page_count, page_len, kv_heads, head_dim = key_cache.shape
    query_width = w_query.shape[1]
    head_count = query_width // head_dim
    floated = hidden.astype(jnp.float32)
    squares = jnp.sum(floated * floated, axis=-1).reshape(row_count, 1)
    normed = (
        (floated * norm_gain.astype(jnp.float32))
        .astype(jnp.bfloat16)
        .reshape(row_count, width_local)
    )
    query_part = jnp.dot(normed, w_query, preferred_element_type=jnp.float32)
    key_part = jnp.dot(normed, w_key, preferred_element_type=jnp.float32)
    value_part = jnp.dot(normed, w_value, preferred_element_type=jnp.float32)
    query_sum, key_sum, value_sum, square_sum = lax.psum(
        (query_part, key_part, value_part, squares), "ctx"
    )
    inv_rms = lax.rsqrt(square_sum / D + epsilon)
    query_heads = (
        (query_sum * inv_rms)
        .astype(jnp.bfloat16)
        .reshape(steps_n, batch_size, kv_heads, head_count // kv_heads, head_dim)
    )
    key_heads = (
        (key_sum * inv_rms).astype(jnp.bfloat16).reshape(steps_n, batch_size, kv_heads, head_dim)
    )
    value_heads = (
        (value_sum * inv_rms).astype(jnp.bfloat16).reshape(steps_n, batch_size, kv_heads, head_dim)
    )
    device = lax.axis_index("ctx")
    local_parts = page_partials(
        query_heads,
        key_cache,
        value_cache,
        retrieval,
        page_table,
        lengths,
        window_start,
        device * page_count,
    )
    fresh_parts = fresh_partials(query_heads, key_heads, value_heads)
    col_share = query_width // lax.axis_size("ctx")
    col_start = device * col_share
    merged = merged_2(local_parts, "ctx", combine)
    highest, totals, summed = combine(merged, fresh_parts)
    attended_full = (
        (summed / totals[..., None]).reshape(row_count, query_width).astype(jnp.bfloat16)
    )
    attended = lax.dynamic_slice_in_dim(attended_full, col_start, col_share, 1)
    partial_out = jnp.dot(attended, w_output, preferred_element_type=jnp.float32)
    reduced = lax.psum_scatter(partial_out, "ctx", scatter_dimension=1, tiled=True)
    return reduced.reshape(steps_n, batch_size, -1).astype(jnp.bfloat16)


log2_e = 1.4426950408889634
chips = 8
far_away = 2**30


def fused(
    n,
    steps_n,
    batch,
    page_len,
    retrieval_hbm,
    lengths_hbm,
    window_hbm,
    hidden_hbm,
    gain_hbm,
    table_hbm,
    wq_hbm,
    wk_hbm,
    wv_hbm,
    wo_hbm,
    keys_hbm,
    values_hbm,
    out_ref,
    retrieval_ref,
    lengths_ref,
    window_ref,
    hidden_ref,
    gain_ref,
    table_ref,
    wq_v,
    wkv_v,
    wo_v,
    keys_v,
    values_v,
    keys_t,
    values_k,
    apart,
    bias,
    msg1,
    twin1,
    recv1,
    fresh_kv,
    gath,
    part3,
    twin3,
    msg3,
    recv3,
    out_own,
    out_other,
    twin4,
    recv4,
    load_sem,
    send_sem,
    recv_sem,
):
    f32, bf16 = jnp.float32, jnp.bfloat16
    me = lax.axis_index("ctx")
    chip, core = me // 2, lax.rem(me, 2)
    other = 1 - core
    pages = keys_v.shape[0]
    dim = 128
    rows = steps_n * batch
    heads_own = 4
    q_rows = heads_own * rows
    share = heads_own * dim
    width_local = hidden_ref.shape[2]
    scale = dim ** (-0.5) * log2_e

    def chip_at(i):
        return lax.rem(chip + i, chips)

    def chip_from(i):
        return lax.rem(chip + chips - i, chips)

    def peer(i):
        return 2 * chip_at(i) + core

    twin = 2 * chip + other

    def load(k, from_ref, to_ref):
        return pltpu.make_async_copy(from_ref, to_ref, load_sem.at[k])

    def remote(phase, i, from_ref, to_ref, device):
        return pltpu.make_async_remote_copy(
            src_ref=from_ref,
            dst_ref=to_ref,
            send_sem=send_sem.at[phase, i],
            recv_sem=recv_sem.at[phase, i],
            device_id={"ctx": device},
            device_id_type=pl.DeviceIdType.MESH,
        )

    kv_width = wk_hbm.shape[1]
    quarter = wq_hbm.shape[1] // 4
    some = pages // 4
    load_kv = [
        load(0, wk_hbm, wkv_v.at[:, pl.ds(0, kv_width)]),
        load(1, wv_hbm, wkv_v.at[:, pl.ds(kv_width, kv_width)]),
    ]
    columns = [pl.ds(j * quarter, quarter) for j in range(4)]
    load_wq = [load(2 + j, wq_hbm.at[:, c], wq_v.at[:, c]) for j, c in enumerate(columns)]
    load_wo = [load(6 + j, wo_hbm.at[:, c], wo_v.at[:, c]) for j, c in enumerate(columns)]
    page_sets = [pl.ds(j * some, some) for j in range(4)]
    load_keys = [load(10 + j, keys_hbm.at[c], keys_v.at[c]) for j, c in enumerate(page_sets)]
    load_values = [load(14 + j, values_hbm.at[c], values_v.at[c]) for j, c in enumerate(page_sets)]

    barrier = pltpu.get_barrier_semaphore()

    def greet(device):
        pl.semaphore_signal(
            barrier, inc=1, device_id={"ctx": device}, device_id_type=pl.DeviceIdType.MESH
        )

    @pl.loop(1, chips)
    def _(i):
        greet(peer(i))

    greet(twin)

    load_small = [
        load(18 + j, from_ref, to_ref)
        for j, (from_ref, to_ref) in enumerate(
            (
                (hidden_hbm, hidden_ref),
                (gain_hbm, gain_ref),
                (table_hbm, table_ref),
                (lengths_hbm, lengths_ref),
                (window_hbm, window_ref),
                (retrieval_hbm, retrieval_ref),
            )
        )
    ]
    for copy in load_small + load_kv + load_wq:
        copy.start()
    for copy in load_small:
        copy.wait()

    loaded = hidden_ref[...].astype(f32)
    floated = jnp.concatenate(
        [loaded[s, b : b + 1, :] for b in range(batch) for s in range(steps_n)], axis=0
    )
    squares = jnp.sum(floated * floated, axis=1, keepdims=True)
    squares = jnp.broadcast_to(squares, (rows, dim))
    normed = (floated * gain_ref[...].astype(f32).reshape(1, width_local)).astype(bf16)

    sub = lax.broadcasted_iota(jnp.int32, (rows, dim), 0)
    lane = lax.broadcasted_iota(jnp.int32, (rows, dim), 1)
    first = sub < steps_n
    table = table_ref[...]
    page_id = lax.broadcasted_iota(jnp.int32, (pages, table.shape[1]), 0) + me * pages
    block = lax.broadcasted_iota(jnp.int32, (pages, table.shape[1]), 1).astype(f32)
    starts = []
    for b in range(batch):
        hit = jnp.where(table[b : b + 1, :] == page_id, 1.0, 0.0)
        found = jnp.sum(hit, axis=1, keepdims=True)
        start = jnp.sum(hit * block, axis=1, keepdims=True) * float(page_len)
        start = jnp.where(found > 0.0, start, float(far_away))
        starts.append(jnp.broadcast_to(start, (pages, dim)).astype(jnp.int32))
    until = jnp.where(first, lengths_ref[0], lengths_ref[1])
    since = jnp.where(first, window_ref[0], window_ref[1])
    for p in range(pages):
        position = jnp.where(first, starts[0][p : p + 1, :], starts[1][p : p + 1, :]) + lane
        cached = position < until
        recent = cached & ((position < SINKS) | (position >= since))
        bias[0, :, pl.ds(p * dim, dim)] = jnp.where(recent, 0.0, very_low)
        bias[1, :, pl.ds(p * dim, dim)] = jnp.where(cached, 0.0, very_low)

    for copy in load_kv:
        copy.wait()
    fresh = jnp.dot(normed, wkv_v[...], preferred_element_type=f32)
    for j in range(chips):
        slot = lax.rem(j + chips - chip, chips)
        for c in range(2):
            at = c * kv_width + j * dim
            msg1[c, slot, pl.ds(q_rows, rows), :] = fresh[:, at : at + dim]
            msg1[c, slot, pl.ds(q_rows + rows, rows), :] = squares
    for j in range(chips):
        if j % 2 == 0:
            load_wq[j // 2].wait()
        if j == 0:
            for copy in load_keys + load_values + load_wo:
                copy.start()
        slot = lax.rem(j + chips - chip, chips)
        query = jnp.dot(
            normed, wq_v[:, pl.ds(j * 2 * share, 2 * share)], preferred_element_type=f32
        )
        for c in range(2):
            for g in range(heads_own):
                at = c * share + g * dim
                msg1[c, slot, pl.ds(g * rows, rows), :] = query[:, at : at + dim]

    pl.semaphore_wait(barrier, chips)

    remote(0, 0, msg1.at[other], twin1, twin).start()
    remote(0, 0, msg1.at[other], twin1, twin).wait_recv()

    @pl.loop(1, chips)
    def _(i):
        msg1[core, i] = msg1[core, i] + twin1[i]
        remote(0, i, msg1.at[core, i], recv1.at[i], peer(i)).start()

    def by_head(p, slot, from_ref):
        apart[slot] = from_ref[p].astype(f32)
        return [apart[slot, pl.ds(k, page_len, stride=chips), :] for k in range(chips)]

    def turn_keys(p, slot):
        at = pl.ds(pl.multiple_of(p * page_len, page_len), page_len)
        for k, part in enumerate(by_head(p, slot, keys_v)):
            keys_t[k, :, at] = part.T.astype(bf16)

    def sort_values(p, slot):
        at = pl.ds(pl.multiple_of(p * page_len, page_len), page_len)
        for k, part in enumerate(by_head(p, slot, values_v)):
            values_k[k, at, :] = part.astype(bf16)

    for copy in load_keys:
        copy.wait()

    @pl.loop(0, pages // 2)
    def _(h):
        for u in range(2):
            turn_keys(2 * h + u, u)

    for copy in load_values:
        copy.wait()

    values_early = pages // 4

    @pl.loop(0, values_early)
    def _(h):
        for u in range(2):
            sort_values(2 * h + u, u)

    def add_far(i, acc):
        remote(0, i, msg1.at[core, i], recv1.at[i], peer(i)).wait_recv()
        return acc + recv1[i]

    summed = lax.fori_loop(1, chips, add_far, msg1[core, 0] + twin1[0])
    inv_rms = lax.rsqrt(summed[q_rows + rows :] / (width_local * n) + epsilon)
    fresh_kv[core] = (summed[q_rows : q_rows + rows] * inv_rms).astype(bf16).astype(f32)
    for g in range(heads_own):
        piece = summed[g * rows : (g + 1) * rows] * inv_rms
        gath[0, core, pl.ds(g * rows, rows), :] = piece.astype(bf16).astype(f32)

    own = gath.at[0, core]

    @pl.loop(1, chips)
    def _(i):
        remote(1, i, own, gath.at[i, core], peer(i)).start()

    remote(2, 0, own, own, twin).start()
    remote(3, 0, fresh_kv.at[core], fresh_kv.at[core], twin).start()

    @pl.loop(values_early, pages // 2)
    def _(h):
        for u in range(2):
            sort_values(2 * h + u, u)

    @pl.loop(1, chips)
    def _(i):
        block = gath.at[i, core]
        remote(1, i, own, block, peer(i)).wait_recv()
        remote(2, i, block, block, twin).start()

    def scores_of(i):
        k = chip_from(i)
        query = gath[i].reshape(2 * q_rows, dim).astype(bf16)
        scores = jnp.dot(query, keys_t[k], preferred_element_type=f32)
        hidden_by = bias[retrieval_ref[k]]
        scores = scores.reshape(2 * heads_own, rows, pages * page_len) * scale + hidden_by[None]
        return scores.reshape(2 * q_rows, pages * page_len)

    def fold(op, wide):
        parts = [wide[:, p * dim : (p + 1) * dim] for p in range(pages)]
        while len(parts) > 1:
            parts = [op(a, b) for a, b in zip(parts[::2], parts[1::2])]
        return parts[0]

    def weigh(scores):
        highest = jnp.max(fold(jnp.maximum, scores), axis=1, keepdims=True)
        weights = jnp.exp2(scores - highest)
        total = jnp.sum(fold(jnp.add, weights), axis=1, keepdims=True)
        return highest, total, weights.astype(bf16)

    def attend(offsets):
        scored = [scores_of(i) for i in offsets]
        weighed = [weigh(scores) for scores in scored]
        summed_up = [
            jnp.dot(weights, values_k[chip_from(i)], preferred_element_type=f32)
            for i, (_, _, weights) in zip(offsets, weighed)
        ]
        for i, summed, (highest, total, _) in zip(offsets, summed_up, weighed):
            highest = jnp.broadcast_to(highest, summed.shape)
            total = jnp.broadcast_to(total, summed.shape)
            for c in range(2):
                mine = slice(c * q_rows, (c + 1) * q_rows)
                part3[i, c, pl.ds(0, q_rows), :] = summed[mine]
                part3[i, c, pl.ds(q_rows, q_rows), :] = highest[mine]
                part3[i, c, pl.ds(2 * q_rows, q_rows), :] = total[mine]
        for i in offsets:
            remote(3, 1 + i, part3.at[i, other], twin3.at[i], twin).start()

    row = lax.broadcasted_iota(jnp.int32, (q_rows, dim), 0)
    col = lax.broadcasted_iota(jnp.int32, (q_rows, dim), 1)

    def join(i):
        remote(3, 1 + i, part3.at[i, other], twin3.at[i], twin).wait_recv()
        a, b = part3[i, core], twin3[i]
        top_a, top_b = a[q_rows : 2 * q_rows], b[q_rows : 2 * q_rows]
        top = jnp.maximum(top_a, top_b)
        factor_a, factor_b = jnp.exp2(top_a - top), jnp.exp2(top_b - top)
        summed = a[:q_rows] * factor_a + b[:q_rows] * factor_b
        total = a[2 * q_rows :] * factor_a + b[2 * q_rows :] * factor_b
        stats = jnp.where(col == row, top, 0.0) + jnp.where(col == row + q_rows, total, 0.0)
        stats = jnp.sum(stats, axis=0, keepdims=True)
        return summed, jnp.broadcast_to(stats, (rows, dim))

    def pass_on(i):
        summed, stats = join(i)
        msg3[i, pl.ds(0, q_rows), :] = summed
        msg3[i, pl.ds(q_rows, rows), :] = stats
        remote(4, i, msg3.at[i], recv3.at[i], peer(chips - i)).start()

    def arrived(i):
        origin = gath.at[i, other]
        remote(2, i, origin, origin, twin).wait_recv()

    arrived(0)
    remote(3, 0, fresh_kv.at[other], fresh_kv.at[other], twin).wait_recv()
    arrived(1)
    attend([0, 1])
    summed, stats = join(0)
    recv3[0, pl.ds(0, q_rows), :] = summed
    recv3[0, pl.ds(q_rows, rows), :] = stats

    @pl.loop(1, chips // 2)
    def _(h):
        arrived(2 * h)
        arrived(2 * h + 1)
        attend([2 * h, 2 * h + 1])

        @pl.when(h > 1)
        def _():
            pass_on(2 * h - 2)

        pass_on(2 * h - 1)

    pass_on(chips - 2)
    pass_on(chips - 1)

    new_key = jnp.concatenate([fresh_kv[0]] * (dim // rows), axis=0).astype(bf16)
    new_value = jnp.concatenate([fresh_kv[1]] * (dim // rows), axis=0).astype(bf16)
    scores = lax.dot_general(
        gath[0, core].astype(bf16), new_key, (((1,), (1,)), ((), ())), preferred_element_type=f32
    )
    token = lax.rem(row, rows)
    causal = (col < rows) & (col // steps_n == token // steps_n) & (col <= token)
    scores = jnp.where(causal, scores * scale, very_low)
    fresh_top = jnp.max(scores, axis=1, keepdims=True)
    weights = jnp.where(causal, jnp.exp2(scores - fresh_top), 0.0)
    fresh_total = jnp.sum(weights, axis=1, keepdims=True)
    fresh_sum = jnp.dot(weights.astype(bf16), new_value, preferred_element_type=f32)

    for copy in load_wo:
        copy.wait()

    @pl.loop(1, chips)
    def _(i):
        remote(4, i, msg3.at[i], recv3.at[i], peer(chips - i)).wait_recv()

    stats = jnp.zeros((rows, dim), f32)
    for i in range(chips):
        stats = jnp.where(sub == i, recv3[i, pl.ds(q_rows, rows), :], stats)
    stats = jnp.concatenate([stats] * (dim // rows), axis=0).T
    top = jnp.where(col < chips, stats[:q_rows], jnp.where(col == chips, fresh_top, very_low))
    total = jnp.where(
        col < chips, stats[q_rows : 2 * q_rows], jnp.where(col == chips, fresh_total, 0.0)
    )
    factor = jnp.exp2(top - jnp.max(top, axis=1, keepdims=True))
    factor = factor / jnp.sum(factor * total, axis=1, keepdims=True)
    acc = fresh_sum * factor[:, chips : chips + 1]
    for i in range(chips):
        acc += recv3[i, pl.ds(0, q_rows), :] * factor[:, i : i + 1]
    attended = jnp.concatenate(
        [acc[g * rows : (g + 1) * rows] for g in range(heads_own)], axis=1
    ).astype(bf16)

    def project_out(j, c):
        at = pl.multiple_of(j * 2 * share + c * share, share)
        return jnp.dot(attended, wo_v[:, pl.ds(at, share)], preferred_element_type=f32)

    for j in range(chips):
        out_other[lax.rem(j + chips - chip, chips)] = project_out(j, other)
    remote(5, 0, out_other, twin4, twin).start()
    for j in range(chips):
        out_own[lax.rem(j + chips - chip, chips)] = project_out(j, core)
    remote(5, 0, out_other, twin4, twin).wait_recv()

    @pl.loop(1, chips)
    def _(i):
        out_own[i] = out_own[i] + twin4[i]
        remote(5, i, out_own.at[i], recv4.at[i], peer(i)).start()

    def add_out(i, acc):
        remote(5, i, out_own.at[i], recv4.at[i], peer(i)).wait_recv()
        return acc + recv4[i]

    result = lax.fori_loop(1, chips, add_out, out_own[0] + twin4[0])
    for s in range(steps_n):
        out_ref[s] = jnp.concatenate(
            [result[b * steps_n + s : b * steps_n + s + 1] for b in range(batch)], axis=0
        ).astype(out_ref.dtype)

    remote(0, 0, msg1.at[other], twin1, twin).wait_send()
    remote(2, 0, own, own, twin).wait_send()
    remote(3, 0, fresh_kv.at[core], fresh_kv.at[core], twin).wait_send()
    remote(3, 1, part3.at[0, other], twin3.at[0], twin).wait_send()
    remote(5, 0, out_other, twin4, twin).wait_send()

    @pl.loop(1, chips)
    def _(i):
        remote(0, i, msg1.at[core, i], recv1.at[i], peer(i)).wait_send()
        remote(1, i, own, gath.at[i, core], peer(i)).wait_send()
        remote(2, i, gath.at[i, core], gath.at[i, core], twin).wait_send()
        remote(3, 1 + i, part3.at[i, other], twin3.at[i], twin).wait_send()
        remote(4, i, msg3.at[i], recv3.at[i], peer(chips - i)).wait_send()
        remote(5, i, out_own.at[i], recv4.at[i], peer(i)).wait_send()


def local(
    hidden,
    norm_gain,
    w_query,
    w_key,
    w_value,
    w_output,
    key_cache,
    value_cache,
    retrieval,
    page_table,
    lengths,
    window_start,
):
    n = lax.axis_size("ctx")
    steps_n, batch, width_local = hidden.shape
    pages, page_len, kv_heads, dim = key_cache.shape
    query_width = w_query.shape[1]
    share = query_width // n
    rows = steps_n * batch
    q_rows = query_width // dim * steps_n
    if pages % 4 or (n, share, rows, batch, kv_heads, dim, page_len) != (16, 512, 8, 2, 8, 128, 128):
        return local_small(
            hidden,
            norm_gain,
            w_query,
            w_key,
            w_value,
            w_output,
            key_cache,
            value_cache,
            retrieval,
            page_table,
            lengths,
            window_start,
        )
    f32, bf16 = jnp.float32, jnp.bfloat16
    vmem = pl.BlockSpec(memory_space=pltpu.VMEM)
    hbm = pl.BlockSpec(memory_space=pl.ANY)
    dma = pltpu.SemaphoreType.DMA
    positions = pages * page_len
    out = pl.pallas_call(
        functools.partial(fused, n, steps_n, batch, page_len),
        out_shape=jax.ShapeDtypeStruct((steps_n, batch, w_output.shape[1] // n), bf16),
        in_specs=[hbm] * 12,
        out_specs=vmem,
        scratch_shapes=[
            pltpu.SMEM(retrieval.shape, jnp.int32),
            pltpu.SMEM(lengths.shape, jnp.int32),
            pltpu.SMEM(window_start.shape, jnp.int32),
            pltpu.VMEM(hidden.shape, bf16),
            pltpu.VMEM(norm_gain.shape, bf16),
            pltpu.VMEM(page_table.shape, jnp.int32),
            pltpu.VMEM((width_local, query_width), bf16),
            pltpu.VMEM((width_local, 2 * kv_heads * dim), bf16),
            pltpu.VMEM((share, w_output.shape[1]), bf16),
            pltpu.VMEM((pages, page_len * kv_heads, dim), bf16),
            pltpu.VMEM((pages, page_len * kv_heads, dim), bf16),
            pltpu.VMEM((kv_heads, dim, positions), bf16),
            pltpu.VMEM((kv_heads, positions, dim), bf16),
            pltpu.VMEM((2, page_len * kv_heads, dim), f32),
            pltpu.VMEM((2, rows, positions), f32),
            pltpu.VMEM((2, chips, 48, dim), f32),
            pltpu.VMEM((chips, 48, dim), f32),
            pltpu.VMEM((chips, 48, dim), f32),
            pltpu.VMEM((2, rows, dim), f32),
            pltpu.VMEM((chips, 2, 32, dim), f32),
            pltpu.VMEM((chips, 2, 96, dim), f32),
            pltpu.VMEM((chips, 96, dim), f32),
            pltpu.VMEM((chips, 40, dim), f32),
            pltpu.VMEM((chips, 40, dim), f32),
            pltpu.VMEM((chips, rows, share), f32),
            pltpu.VMEM((chips, rows, share), f32),
            pltpu.VMEM((chips, rows, share), f32),
            pltpu.VMEM((chips, rows, share), f32),
            dma((24,)),
            dma((6, chips + 1)),
            dma((6, chips + 1)),
        ],
        compiler_params=pltpu.CompilerParams(
            collective_id=0, has_side_effects=True, vmem_limit_bytes=56 * 2**20
        ),
    )(
        retrieval,
        lengths,
        window_start,
        hidden,
        norm_gain,
        page_table,
        w_query,
        w_key,
        w_value,
        w_output,
        key_cache.reshape(pages, page_len * kv_heads, dim),
        value_cache.reshape(pages, page_len * kv_heads, dim),
    )
    return out


def solution(mesh):
    placed = (
        P(None, "groups", "ctx"),
        P("ctx"),
        P("ctx", None),
        P("ctx", None),
        P("ctx", None),
        P("ctx", None),
        P(("groups", "ctx"), None, None, None),
        P(("groups", "ctx"), None, None, None),
        P(),
        P("groups", None),
        P("groups"),
        P("groups"),
    )
    return jax.shard_map(
        local, mesh=mesh, in_specs=placed, out_specs=P(None, "groups", "ctx"), check_vma=False
    )
```

```python
import functools

import jax
import jax.numpy as jnp
from jax import lax
from jax.experimental import pallas as pl
from jax.experimental.pallas import tpu as pltpu
from jax.sharding import PartitionSpec as P

D = 8192
SINKS = 4


very_low = -1e30
epsilon = 1e-05


def merged_2(shard, axis, combine):
    everything = jax.tree.map(lambda part: lax.all_gather(part, axis), shard)
    first = jax.tree.map(lambda part: part[0], everything)

    def turn(k, so_far):
        return combine(so_far, jax.tree.map(lambda part: part[k], everything))

    return lax.fori_loop(1, lax.axis_size(axis), turn, first)


def combine(earlier, later):
    top_a, total_a, summed_a = earlier
    top_b, total_b, summed_b = later
    highest = jnp.maximum(top_a, top_b)
    factor_a = jnp.exp(top_a - highest)
    factor_b = jnp.exp(top_b - highest)
    return (
        highest,
        total_a * factor_a + total_b * factor_b,
        summed_a * factor_a[..., None] + summed_b * factor_b[..., None],
    )


def arrange(top_val, total_val, summed_val, row_count):
    head_count = top_val.shape[1] * top_val.shape[2]
    top_val = jnp.transpose(top_val, (3, 0, 1, 2)).reshape(row_count, head_count)
    total_val = jnp.transpose(total_val, (3, 0, 1, 2)).reshape(row_count, head_count)
    summed_val = jnp.transpose(summed_val, (3, 0, 1, 2, 4)).reshape(
        row_count, head_count, summed_val.shape[-1]
    )
    return (top_val, total_val, summed_val)


def of_owner(values, owner_req, axis):
    picked = None
    for b in range(values.shape[axis]):
        entry = lax.slice_in_dim(values, b, b + 1, axis=axis)
        mine = (owner_req == b).reshape((-1,) + (1,) * (values.ndim - 1 - axis))
        picked = entry if picked is None else jnp.where(mine, entry, picked)
    shape = list(values.shape)
    shape[axis] = owner_req.shape[0]
    return jnp.broadcast_to(picked, shape)


def page_partials(
    query_heads, page_keys, page_values, retrieval, page_table, lengths, window_start, first_page
):
    page_count, page_len, kv_heads, head_dim = page_keys.shape
    batch_size, blocks = page_table.shape
    steps_n = query_heads.shape[0]
    slot_ids = first_page + jnp.arange(page_count, dtype=jnp.int32)
    matches = (page_table[None, :, :] == slot_ids[:, None, None]).astype(jnp.int32)
    owner_req = jnp.sum(
        matches * jnp.arange(batch_size, dtype=jnp.int32)[None, :, None], axis=(1, 2)
    )
    block_ids = jnp.sum(matches * jnp.arange(blocks, dtype=jnp.int32)[None, None, :], axis=(1, 2))
    query_page = of_owner(query_heads, owner_req, 1)
    scores = jnp.einsum(
        "spkgd,ptkd->pkgst", query_page, page_keys, preferred_element_type=jnp.float32
    ) * head_dim ** (-0.5)
    positions = block_ids[:, None] * page_len + jnp.arange(page_len, dtype=jnp.int32)[None, :]
    in_range = positions < of_owner(lengths, owner_req, 0)[:, None]
    recent = (positions < SINKS) | (positions >= of_owner(window_start, owner_req, 0)[:, None])
    visible = in_range[:, None, :] & ((retrieval[None, :, None] == 1) | recent[:, None, :])
    visible = visible[:, :, None, None, :]
    masked = jnp.where(visible, scores, very_low)
    owner_hot = owner_req[:, None] == jnp.arange(batch_size, dtype=jnp.int32)[None, :]
    page_max = jnp.max(masked, axis=-1)
    local_max = jnp.max(
        jnp.where(owner_hot[:, :, None, None, None], page_max[:, None], very_low), axis=0
    )
    row_max = of_owner(local_max, owner_req, 0)
    weights = jnp.where(visible, jnp.exp(masked - row_max[..., None]), 0.0)
    owner_float = owner_hot.astype(jnp.float32)
    local_total = jnp.einsum(
        "pb,pkgs->bkgs", owner_float, jnp.sum(weights, axis=-1), precision=lax.Precision.HIGHEST
    )
    values = jnp.einsum(
        "pkgst,ptkd->pkgsd",
        weights.astype(jnp.bfloat16),
        page_values,
        preferred_element_type=jnp.float32,
    )
    local_sum = jnp.einsum("pb,pkgsd->bkgsd", owner_float, values, precision=lax.Precision.HIGHEST)
    return arrange(local_max, local_total, local_sum, steps_n * batch_size)


def fresh_partials(query_heads, key_heads, value_heads):
    steps_n, batch_size, kv_heads, group, head_dim = query_heads.shape
    scores = jnp.einsum(
        "sbkgd,ubkd->bkgsu", query_heads, key_heads, preferred_element_type=jnp.float32
    ) * head_dim ** (-0.5)
    causal = jnp.arange(steps_n)[:, None] >= jnp.arange(steps_n)[None, :]
    masked = jnp.where(causal, scores, very_low)
    highest = jnp.max(masked, axis=-1)
    weights = jnp.where(causal, jnp.exp(masked - highest[..., None]), 0.0)
    totals = jnp.sum(weights, axis=-1)
    summed = jnp.einsum(
        "bkgsu,ubkd->bkgsd",
        weights.astype(jnp.bfloat16),
        value_heads,
        preferred_element_type=jnp.float32,
    )
    return arrange(highest, totals, summed, steps_n * batch_size)


def local_small(
    hidden,
    norm_gain,
    w_query,
    w_key,
    w_value,
    w_output,
    key_cache,
    value_cache,
    retrieval,
    page_table,
    lengths,
    window_start,
):
    steps_n, batch_size, width_local = hidden.shape
    row_count = steps_n * batch_size
    page_count, page_len, kv_heads, head_dim = key_cache.shape
    query_width = w_query.shape[1]
    head_count = query_width // head_dim
    floated = hidden.astype(jnp.float32)
    squares = jnp.sum(floated * floated, axis=-1).reshape(row_count, 1)
    normed = (
        (floated * norm_gain.astype(jnp.float32))
        .astype(jnp.bfloat16)
        .reshape(row_count, width_local)
    )
    query_part = jnp.dot(normed, w_query, preferred_element_type=jnp.float32)
    key_part = jnp.dot(normed, w_key, preferred_element_type=jnp.float32)
    value_part = jnp.dot(normed, w_value, preferred_element_type=jnp.float32)
    query_sum, key_sum, value_sum, square_sum = lax.psum(
        (query_part, key_part, value_part, squares), "ctx"
    )
    inv_rms = lax.rsqrt(square_sum / D + epsilon)
    query_heads = (
        (query_sum * inv_rms)
        .astype(jnp.bfloat16)
        .reshape(steps_n, batch_size, kv_heads, head_count // kv_heads, head_dim)
    )
    key_heads = (
        (key_sum * inv_rms).astype(jnp.bfloat16).reshape(steps_n, batch_size, kv_heads, head_dim)
    )
    value_heads = (
        (value_sum * inv_rms).astype(jnp.bfloat16).reshape(steps_n, batch_size, kv_heads, head_dim)
    )
    device = lax.axis_index("ctx")
    local_parts = page_partials(
        query_heads,
        key_cache,
        value_cache,
        retrieval,
        page_table,
        lengths,
        window_start,
        device * page_count,
    )
    fresh_parts = fresh_partials(query_heads, key_heads, value_heads)
    col_share = query_width // lax.axis_size("ctx")
    col_start = device * col_share
    merged = merged_2(local_parts, "ctx", combine)
    highest, totals, summed = combine(merged, fresh_parts)
    attended_full = (
        (summed / totals[..., None]).reshape(row_count, query_width).astype(jnp.bfloat16)
    )
    attended = lax.dynamic_slice_in_dim(attended_full, col_start, col_share, 1)
    partial_out = jnp.dot(attended, w_output, preferred_element_type=jnp.float32)
    reduced = lax.psum_scatter(partial_out, "ctx", scatter_dimension=1, tiled=True)
    return reduced.reshape(steps_n, batch_size, -1).astype(jnp.bfloat16)


log2_e = 1.4426950408889634
chips = 8
far_away = 2**30


def fused(
    n,
    steps_n,
    batch,
    page_len,
    retrieval_hbm,
    lengths_hbm,
    window_hbm,
    hidden_hbm,
    gain_hbm,
    table_hbm,
    wq_hbm,
    wk_hbm,
    wv_hbm,
    wo_hbm,
    keys_hbm,
    values_hbm,
    out_ref,
    retrieval_ref,
    lengths_ref,
    window_ref,
    hidden_ref,
    gain_ref,
    table_ref,
    wq_v,
    wkv_v,
    wo_v,
    keys_v,
    values_v,
    keys_t,
    values_k,
    apart,
    bias,
    msg1,
    twin1,
    recv1,
    fresh_kv,
    gath,
    part3,
    twin3,
    msg3,
    recv3,
    out_own,
    out_other,
    twin4,
    recv4,
    load_sem,
    send_sem,
    recv_sem,
):
    f32, bf16 = jnp.float32, jnp.bfloat16
    me = lax.axis_index("ctx")
    chip, core = me // 2, lax.rem(me, 2)
    other = 1 - core
    pages = keys_v.shape[0]
    dim = 128
    rows = steps_n * batch
    heads_own = 4
    q_rows = heads_own * rows
    share = heads_own * dim
    width_local = hidden_ref.shape[2]
    scale = dim ** (-0.5) * log2_e

    def apart_by(a, b):
        where = 0
        for bit in (1, 2, 4):
            p, q = lax.rem(a // bit, 2), (b // bit) % 2
            where = where + bit * (p + q - 2 * p * q)
        return where

    def chip_at(i):
        return apart_by(chip, i)

    def peer(i, c=None):
        return 2 * chip_at(i) + (core if c is None else c)

    def in_turn(t):
        return apart_by(chip, lax.rem(chip + t, chips))

    far_in = 6

    twin = 2 * chip + other

    def load(k, from_ref, to_ref):
        return pltpu.make_async_copy(from_ref, to_ref, load_sem.at[k])

    sums_twin, sums_far, kv_twin, parts_far, outs_twin, outs_far = range(6)
    query_far, query_twin, parts_twin = range(6, 9)

    def remote(kind, i, from_ref, to_ref, device):
        return pltpu.make_async_remote_copy(
            src_ref=from_ref,
            dst_ref=to_ref,
            send_sem=send_sem.at[kind],
            recv_sem=recv_sem.at[kind if kind < 6 else 6 + chips * (kind - 6) + i],
            device_id={"ctx": device},
            device_id_type=pl.DeviceIdType.MESH,
        )

    kv_width = wk_hbm.shape[1]
    quarter = wq_hbm.shape[1] // 4
    load_kv = [
        load(0, wk_hbm, wkv_v.at[:, pl.ds(0, kv_width)]),
        load(0, wv_hbm, wkv_v.at[:, pl.ds(kv_width, kv_width)]),
    ]
    load_wo = load(1, wo_hbm, wo_v)
    load_keys = load(2, keys_hbm, keys_v)
    load_values = load(3, values_hbm, values_v)
    columns = [pl.ds(j * quarter, quarter) for j in range(4)]
    load_wq = [load(4 + j, wq_hbm.at[:, c], wq_v.at[:, c]) for j, c in enumerate(columns)]

    barrier = pltpu.get_barrier_semaphore()

    def greet(device):
        pl.semaphore_signal(
            barrier, inc=1, device_id={"ctx": device}, device_id_type=pl.DeviceIdType.MESH
        )

    @pl.loop(1, chips)
    def _(i):
        greet(peer(i))

    greet(twin)


    @pl.loop(far_in, chips)
    def _(i):
        greet(peer(i, other))

    load_small = [
        load(8 + j, from_ref, to_ref)
        for j, (from_ref, to_ref) in enumerate(
            (
                (hidden_hbm, hidden_ref),
                (gain_hbm, gain_ref),
                (table_hbm, table_ref),
                (lengths_hbm, lengths_ref),
                (window_hbm, window_ref),
                (retrieval_hbm, retrieval_ref),
            )
        )
    ]
    for copy in load_small + load_kv + load_wq:
        copy.start()
    for copy in load_small:
        copy.wait()

    loaded = hidden_ref[...].astype(f32)
    floated = jnp.concatenate(
        [loaded[s, b : b + 1, :] for b in range(batch) for s in range(steps_n)], axis=0
    )
    squares = jnp.sum(floated * floated, axis=1, keepdims=True)
    normed = (floated * gain_ref[...].astype(f32).reshape(1, width_local)).astype(bf16)

    sub = lax.broadcasted_iota(jnp.int32, (rows, dim), 0)
    lane = lax.broadcasted_iota(jnp.int32, (rows, dim), 1)
    squares = jnp.sum(jnp.where(lane == sub, squares, 0.0), axis=0, keepdims=True)
    first = sub < steps_n
    table = table_ref[...]
    page_id = lax.broadcasted_iota(jnp.int32, (pages, table.shape[1]), 0) + me * pages
    block = lax.broadcasted_iota(jnp.int32, (pages, table.shape[1]), 1).astype(f32)
    starts = []
    for b in range(batch):
        hit = jnp.where(table[b : b + 1, :] == page_id, 1.0, 0.0)
        found = jnp.sum(hit, axis=1, keepdims=True)
        start = jnp.sum(hit * block, axis=1, keepdims=True) * float(page_len)
        start = jnp.where(found > 0.0, start, float(far_away))
        starts.append(jnp.broadcast_to(start, (pages, dim)).astype(jnp.int32))
    until = jnp.where(first, lengths_ref[0], lengths_ref[1])
    since = jnp.where(first, window_ref[0], window_ref[1])
    for p in range(pages):
        position = jnp.where(first, starts[0][p : p + 1, :], starts[1][p : p + 1, :]) + lane
        cached = position < until
        recent = cached & ((position < SINKS) | (position >= since))
        bias[0, :, pl.ds(p * dim, dim)] = jnp.where(recent, 0.0, very_low)
        bias[1, :, pl.ds(p * dim, dim)] = jnp.where(cached, 0.0, very_low)

    load(0, wkv_v, wkv_v).wait()
    fresh = jnp.dot(normed, wkv_v[...], preferred_element_type=f32)
    for j in range(chips):
        slot = chip_at(j)
        for c in range(2):
            at = c * kv_width + j * dim
            msg1[c, slot, pl.ds(q_rows, rows), :] = fresh[:, at : at + dim]
            msg1[c, slot, pl.ds(q_rows + rows, 1), :] = squares
    for j in range(chips):
        if j % 2 == 0:
            load_wq[j // 2].wait()
        if j == 0:
            for copy in (load_keys, load_values, load_wo):
                copy.start()
        slot = chip_at(j)
        query = jnp.dot(
            normed, wq_v[:, pl.ds(j * 2 * share, 2 * share)], preferred_element_type=f32
        )
        for c in range(2):
            for g in range(heads_own):
                at = c * share + g * dim
                msg1[c, slot, pl.ds(g * rows, rows), :] = query[:, at : at + dim]

    pl.semaphore_wait(barrier, 2 * chips - far_in)

    joined1 = remote(sums_twin, 0, msg1.at[other], twin1, twin)
    joined1.start()
    joined1.wait_recv()

    @pl.loop(1, chips)
    def _(t):
        i = in_turn(t)
        msg1[core, i] = msg1[core, i] + twin1[i]
        remote(sums_far, 0, msg1.at[core, i], recv1.at[i], peer(i)).start()

    def by_head(p, slot, from_ref):
        apart[slot] = from_ref[p].astype(f32)
        return [apart[slot, pl.ds(k, page_len, stride=chips), :] for k in range(chips)]

    def turn_keys(p, slot):
        at = pl.ds(pl.multiple_of(p * page_len, page_len), page_len)
        for k, part in enumerate(by_head(p, slot, keys_v)):
            keys_t[k, :, at] = part.T.astype(bf16)

    def sort_values(p, slot):
        at = pl.ds(pl.multiple_of(p * page_len, page_len), page_len)
        for k, part in enumerate(by_head(p, slot, values_v)):
            values_k[k, at, :] = part.astype(bf16)

    load_keys.wait()

    @pl.loop(0, pages // 2)
    def _(h):
        for u in range(2):
            turn_keys(2 * h + u, u)

    load_values.wait()

    values_early = 3 * pages // 8

    @pl.loop(0, values_early)
    def _(h):
        for u in range(2):
            sort_values(2 * h + u, u)

    all_far = pl.ds(1, chips - 1)
    all1 = remote(sums_far, 0, msg1.at[core, all_far], recv1.at[all_far], twin)
    all1.wait_recv()
    summed = msg1[core, 0] + twin1[0]
    for i in range(1, chips):
        summed = summed + recv1[i]
    squares = jnp.where(lane == sub, summed[q_rows + rows :], 0.0)
    squares = jnp.sum(squares, axis=1, keepdims=True)
    inv_rms = lax.rsqrt(squares / (width_local * n) + epsilon)
    fresh_kv[core] = (summed[q_rows : q_rows + rows] * inv_rms).astype(bf16).astype(f32)
    for g in range(heads_own):
        piece = summed[g * rows : (g + 1) * rows] * inv_rms
        gath[0, core, pl.ds(g * rows, rows), :] = piece.astype(bf16).astype(f32)

    own = gath.at[0, core]

    def query_across(i, device):
        block = gath.at[i if i < far_in else 0, core]
        return remote(query_twin, i, block, gath.at[i, core], device)

    @pl.loop(1, chips)
    def _(t):
        i = in_turn(t)
        remote(query_far, i, own, gath.at[i, core], peer(i)).start()

    query_across(0, twin).start()
    kv_swap = remote(kv_twin, 0, fresh_kv.at[core], fresh_kv.at[core], twin)
    kv_swap.start()
    for i in range(far_in, chips):
        query_across(i, peer(i, other)).start()

    @pl.loop(values_early, pages // 2)
    def _(h):
        for u in range(2):
            sort_values(2 * h + u, u)

    def query_far_in(i):
        remote(query_far, i, own, gath.at[i, core], twin).wait_recv()

    def forward(i):
        query_far_in(i)
        query_across(i, twin).start()

    def arrived(i):
        if i >= far_in:
            query_far_in(i)
        block = gath.at[i, other]
        remote(query_twin, i, block, block, twin).wait_recv()

    def scores_of(i):
        k = chip_at(i)
        query = gath[i].reshape(2 * q_rows, dim).astype(bf16)
        scores = jnp.dot(query, keys_t[k], preferred_element_type=f32)
        hidden_by = bias[retrieval_ref[k]]
        scores = scores.reshape(2 * heads_own, rows, pages * page_len) * scale + hidden_by[None]
        return scores.reshape(2 * q_rows, pages * page_len)

    def fold(op, wide):
        parts = [wide[:, p * dim : (p + 1) * dim] for p in range(pages)]
        while len(parts) > 1:
            parts = [op(a, b) for a, b in zip(parts[::2], parts[1::2])]
        return parts[0]

    def weigh(scores):
        highest = jnp.max(fold(jnp.maximum, scores), axis=1, keepdims=True)
        weights = jnp.exp2(scores - highest)
        total = jnp.sum(fold(jnp.add, weights), axis=1, keepdims=True)
        return highest, total, weights.astype(bf16)

    def attend(offsets):
        scored = [scores_of(i) for i in offsets]
        weighed = [weigh(scores) for scores in scored]
        summed_up = [
            jnp.dot(weights, values_k[chip_at(i)], preferred_element_type=f32)
            for i, (_, _, weights) in zip(offsets, weighed)
        ]
        for i, summed, (highest, total, _) in zip(offsets, summed_up, weighed):
            highest = jnp.broadcast_to(highest, summed.shape)
            total = jnp.broadcast_to(total, summed.shape)
            for c in range(2):
                mine = slice(c * q_rows, (c + 1) * q_rows)
                part3[i, c, pl.ds(0, q_rows), :] = summed[mine]
                part3[i, c, pl.ds(q_rows, q_rows), :] = highest[mine]
                part3[i, c, pl.ds(2 * q_rows, q_rows), :] = total[mine]
        for i in offsets:
            part_swap(i).start()

    def part_swap(i):
        return remote(parts_twin, i, part3.at[i, other], twin3.at[i], twin)

    row = lax.broadcasted_iota(jnp.int32, (q_rows, dim), 0)
    col = lax.broadcasted_iota(jnp.int32, (q_rows, dim), 1)

    def stats_row(top, total):
        stats = jnp.where(col == row, top, 0.0) + jnp.where(col == row + q_rows, total, 0.0)
        return jnp.sum(stats, axis=0, keepdims=True)

    def join(i, to_ref):
        part_swap(i).wait_recv()
        a, b = part3[i, core], twin3[i]
        top_a, top_b = a[q_rows : 2 * q_rows], b[q_rows : 2 * q_rows]
        top = jnp.maximum(top_a, top_b)
        factor_a, factor_b = jnp.exp2(top_a - top), jnp.exp2(top_b - top)
        total = a[2 * q_rows :] * factor_a + b[2 * q_rows :] * factor_b
        to_ref[pl.ds(0, q_rows), :] = a[:q_rows] * factor_a + b[:q_rows] * factor_b
        to_ref[pl.ds(q_rows, 1), :] = stats_row(top, total)

    def pass_on(offsets):
        for i in offsets:
            join(i, msg3.at[i])
            remote(parts_far, 0, msg3.at[i], recv3.at[i], peer(i)).start()

    arrived(0)
    attend([0])
    for i in range(1, 4): forward(i)
    for i in (1,2,3): arrived(i)
    attend([1, 2, 3])
    for i in range(4, 6): forward(i)
    join(0, recv3.at[0])
    for i in (6,7): arrived(i)
    attend([6, 7])
    pass_on((1,2,3))
    for i in (4,5): arrived(i)
    attend([4, 5])
    pass_on((6,7))
    pass_on((4,5))
    remote(kv_twin, 0, fresh_kv.at[other], fresh_kv.at[other], twin).wait_recv()

    new_key = jnp.concatenate([fresh_kv[0]] * (dim // rows), axis=0).astype(bf16)
    new_value = jnp.concatenate([fresh_kv[1]] * (dim // rows), axis=0).astype(bf16)
    scores = lax.dot_general(
        gath[0, core].astype(bf16), new_key, (((1,), (1,)), ((), ())), preferred_element_type=f32
    )
    token = lax.rem(row, rows)
    causal = (col < rows) & (col // steps_n == token // steps_n) & (col <= token)
    scores = jnp.where(causal, scores * scale, very_low)
    fresh_top = jnp.max(scores, axis=1, keepdims=True)
    weights = jnp.where(causal, jnp.exp2(scores - fresh_top), 0.0)
    fresh_total = jnp.sum(weights, axis=1, keepdims=True)
    fresh_sum = jnp.dot(weights.astype(bf16), new_value, preferred_element_type=f32)

    load_wo.wait()

    all3 = remote(parts_far, 0, msg3.at[all_far], recv3.at[all_far], twin)
    all3.wait_recv()

    parts = [recv3.at[i] for i in range(chips)]
    count = len(parts)
    stats = jnp.zeros((rows, dim), f32)
    for k, part in enumerate(parts):
        stats = jnp.where(sub == k, part[pl.ds(q_rows, 1), :], stats)
    stats = jnp.concatenate([stats] * (dim // rows), axis=0).T
    top = jnp.where(col < count, stats[:q_rows], jnp.where(col == count, fresh_top, very_low))
    total = jnp.where(
        col < count, stats[q_rows : 2 * q_rows], jnp.where(col == count, fresh_total, 0.0)
    )
    factor = jnp.exp2(top - jnp.max(top, axis=1, keepdims=True))
    factor = factor / jnp.sum(factor * total, axis=1, keepdims=True)
    acc = fresh_sum * factor[:, count : count + 1]
    for k, part in enumerate(parts):
        acc += part[pl.ds(0, q_rows), :] * factor[:, k : k + 1]
    attended = jnp.concatenate(
        [acc[g * rows : (g + 1) * rows] for g in range(heads_own)], axis=1
    ).astype(bf16)

    def project_out(j, c):
        at = pl.multiple_of((2 * j + c) * share, share)
        return jnp.dot(attended, wo_v[:, pl.ds(at, share)], preferred_element_type=f32)

    for j in range(chips):
        out_other[chip_at(j)] = project_out(j, other)
    joined4 = remote(outs_twin, 0, out_other, twin4, twin)
    joined4.start()
    for j in range(chips):
        out_own[chip_at(j)] = project_out(j, core)
    joined4.wait_recv()

    @pl.loop(1, chips)
    def _(t):
        i = in_turn(t)
        out_own[i] = out_own[i] + twin4[i]
        remote(outs_far, 0, out_own.at[i], recv4.at[i], peer(i)).start()

    all4 = remote(outs_far, 0, out_own.at[all_far], recv4.at[all_far], twin)
    all4.wait_recv()
    result = out_own[0] + twin4[0]
    for i in range(1, chips):
        result = result + recv4[i]
    for s in range(steps_n):
        out_ref[s] = jnp.concatenate(
            [result[b * steps_n + s : b * steps_n + s + 1] for b in range(batch)], axis=0
        ).astype(out_ref.dtype)

    queries_out, queries_on = gath.at[all_far, core], gath.at[:, core]
    swapped = part3.at[:, other]
    for copy in (
        joined1,
        all1,
        remote(query_far, 0, queries_out, queries_out, twin),
        remote(query_twin, 0, queries_on, queries_on, twin),
        kv_swap,
        remote(parts_twin, 0, swapped, swapped, twin),
        all3,
        joined4,
        all4,
    ):
        copy.wait_send()


def local(
    hidden,
    norm_gain,
    w_query,
    w_key,
    w_value,
    w_output,
    key_cache,
    value_cache,
    retrieval,
    page_table,
    lengths,
    window_start,
):
    n = lax.axis_size("ctx")
    steps_n, batch, width_local = hidden.shape
    pages, page_len, kv_heads, dim = key_cache.shape
    query_width = w_query.shape[1]
    share = query_width // n
    rows = steps_n * batch
    q_rows = query_width // dim * steps_n
    if pages % 4 or (n, share, rows, batch, kv_heads, dim, page_len) != (16, 512, 8, 2, 8, 128, 128):
        return local_small(
            hidden,
            norm_gain,
            w_query,
            w_key,
            w_value,
            w_output,
            key_cache,
            value_cache,
            retrieval,
            page_table,
            lengths,
            window_start,
        )
    f32, bf16 = jnp.float32, jnp.bfloat16
    vmem = pl.BlockSpec(memory_space=pltpu.VMEM)
    hbm = pl.BlockSpec(memory_space=pl.ANY)
    dma = pltpu.SemaphoreType.DMA
    positions = pages * page_len
    out = pl.pallas_call(
        functools.partial(fused, n, steps_n, batch, page_len),
        out_shape=jax.ShapeDtypeStruct((steps_n, batch, w_output.shape[1] // n), bf16),
        in_specs=[hbm] * 12,
        out_specs=vmem,
        scratch_shapes=[
            pltpu.SMEM(retrieval.shape, jnp.int32),
            pltpu.SMEM(lengths.shape, jnp.int32),
            pltpu.SMEM(window_start.shape, jnp.int32),
            pltpu.VMEM(hidden.shape, bf16),
            pltpu.VMEM(norm_gain.shape, bf16),
            pltpu.VMEM(page_table.shape, jnp.int32),
            pltpu.VMEM((width_local, query_width), bf16),
            pltpu.VMEM((width_local, 2 * kv_heads * dim), bf16),
            pltpu.VMEM((share, w_output.shape[1]), bf16),
            pltpu.VMEM((pages, page_len * kv_heads, dim), bf16),
            pltpu.VMEM((pages, page_len * kv_heads, dim), bf16),
            pltpu.VMEM((kv_heads, dim, positions), bf16),
            pltpu.VMEM((kv_heads, positions, dim), bf16),
            pltpu.VMEM((2, page_len * kv_heads, dim), f32),
            pltpu.VMEM((2, rows, positions), f32),
            pltpu.VMEM((2, chips, 41, dim), f32),
            pltpu.VMEM((chips, 41, dim), f32),
            pltpu.VMEM((chips, 41, dim), f32),
            pltpu.VMEM((2, rows, dim), f32),
            pltpu.VMEM((chips, 2, 32, dim), f32),
            pltpu.VMEM((chips, 2, 96, dim), f32),
            pltpu.VMEM((chips, 96, dim), f32),
            pltpu.VMEM((chips, 33, dim), f32),
            pltpu.VMEM((chips, 33, dim), f32),
            pltpu.VMEM((chips, rows, share), f32),
            pltpu.VMEM((chips, rows, share), f32),
            pltpu.VMEM((chips, rows, share), f32),
            pltpu.VMEM((chips, rows, share), f32),
            dma((14,)),
            dma((9,)),
            dma((6 + 3 * chips,)),
        ],
        compiler_params=pltpu.CompilerParams(
            collective_id=0, has_side_effects=True, vmem_limit_bytes=56 * 2**20
        ),
    )(
        retrieval,
        lengths,
        window_start,
        hidden,
        norm_gain,
        page_table,
        w_query,
        w_key,
        w_value,
        w_output,
        key_cache.reshape(pages, page_len * kv_heads, dim),
        value_cache.reshape(pages, page_len * kv_heads, dim),
    )
    return out


def solution(mesh):
    placed = (
        P(None, "groups", "ctx"),
        P("ctx"),
        P("ctx", None),
        P("ctx", None),
        P("ctx", None),
        P("ctx", None),
        P(("groups", "ctx"), None, None, None),
        P(("groups", "ctx"), None, None, None),
        P(),
        P("groups", None),
        P("groups"),
        P("groups"),
    )
    return jax.shard_map(
        local, mesh=mesh, in_specs=placed, out_specs=P(None, "groups", "ctx"), check_vma=False
    )
```

```python
import functools

import jax
import jax.numpy as jnp
from jax import lax
from jax.experimental import pallas as pl
from jax.experimental.pallas import tpu as pltpu
from jax.sharding import PartitionSpec as P

D = 8192
SINKS = 4


very_low = -1e30
epsilon = 1e-05


def merged_2(shard, axis, combine):
    everything = jax.tree.map(lambda part: lax.all_gather(part, axis), shard)
    first = jax.tree.map(lambda part: part[0], everything)

    def turn(k, so_far):
        return combine(so_far, jax.tree.map(lambda part: part[k], everything))

    return lax.fori_loop(1, lax.axis_size(axis), turn, first)


def combine(earlier, later):
    top_a, total_a, summed_a = earlier
    top_b, total_b, summed_b = later
    highest = jnp.maximum(top_a, top_b)
    factor_a = jnp.exp(top_a - highest)
    factor_b = jnp.exp(top_b - highest)
    return (
        highest,
        total_a * factor_a + total_b * factor_b,
        summed_a * factor_a[..., None] + summed_b * factor_b[..., None],
    )


def arrange(top_val, total_val, summed_val, row_count):
    head_count = top_val.shape[1] * top_val.shape[2]
    top_val = jnp.transpose(top_val, (3, 0, 1, 2)).reshape(row_count, head_count)
    total_val = jnp.transpose(total_val, (3, 0, 1, 2)).reshape(row_count, head_count)
    summed_val = jnp.transpose(summed_val, (3, 0, 1, 2, 4)).reshape(
        row_count, head_count, summed_val.shape[-1]
    )
    return (top_val, total_val, summed_val)


def of_owner(values, owner_req, axis):
    picked = None
    for b in range(values.shape[axis]):
        entry = lax.slice_in_dim(values, b, b + 1, axis=axis)
        mine = (owner_req == b).reshape((-1,) + (1,) * (values.ndim - 1 - axis))
        picked = entry if picked is None else jnp.where(mine, entry, picked)
    shape = list(values.shape)
    shape[axis] = owner_req.shape[0]
    return jnp.broadcast_to(picked, shape)


def page_partials(
    query_heads, page_keys, page_values, retrieval, page_table, lengths, window_start, first_page
):
    page_count, page_len, kv_heads, head_dim = page_keys.shape
    batch_size, blocks = page_table.shape
    steps_n = query_heads.shape[0]
    slot_ids = first_page + jnp.arange(page_count, dtype=jnp.int32)
    matches = (page_table[None, :, :] == slot_ids[:, None, None]).astype(jnp.int32)
    owner_req = jnp.sum(
        matches * jnp.arange(batch_size, dtype=jnp.int32)[None, :, None], axis=(1, 2)
    )
    block_ids = jnp.sum(matches * jnp.arange(blocks, dtype=jnp.int32)[None, None, :], axis=(1, 2))
    query_page = of_owner(query_heads, owner_req, 1)
    scores = jnp.einsum(
        "spkgd,ptkd->pkgst", query_page, page_keys, preferred_element_type=jnp.float32
    ) * head_dim ** (-0.5)
    positions = block_ids[:, None] * page_len + jnp.arange(page_len, dtype=jnp.int32)[None, :]
    in_range = positions < of_owner(lengths, owner_req, 0)[:, None]
    recent = (positions < SINKS) | (positions >= of_owner(window_start, owner_req, 0)[:, None])
    visible = in_range[:, None, :] & ((retrieval[None, :, None] == 1) | recent[:, None, :])
    visible = visible[:, :, None, None, :]
    masked = jnp.where(visible, scores, very_low)
    owner_hot = owner_req[:, None] == jnp.arange(batch_size, dtype=jnp.int32)[None, :]
    page_max = jnp.max(masked, axis=-1)
    local_max = jnp.max(
        jnp.where(owner_hot[:, :, None, None, None], page_max[:, None], very_low), axis=0
    )
    row_max = of_owner(local_max, owner_req, 0)
    weights = jnp.where(visible, jnp.exp(masked - row_max[..., None]), 0.0)
    owner_float = owner_hot.astype(jnp.float32)
    local_total = jnp.einsum(
        "pb,pkgs->bkgs", owner_float, jnp.sum(weights, axis=-1), precision=lax.Precision.HIGHEST
    )
    values = jnp.einsum(
        "pkgst,ptkd->pkgsd",
        weights.astype(jnp.bfloat16),
        page_values,
        preferred_element_type=jnp.float32,
    )
    local_sum = jnp.einsum("pb,pkgsd->bkgsd", owner_float, values, precision=lax.Precision.HIGHEST)
    return arrange(local_max, local_total, local_sum, steps_n * batch_size)


def fresh_partials(query_heads, key_heads, value_heads):
    steps_n, batch_size, kv_heads, group, head_dim = query_heads.shape
    scores = jnp.einsum(
        "sbkgd,ubkd->bkgsu", query_heads, key_heads, preferred_element_type=jnp.float32
    ) * head_dim ** (-0.5)
    causal = jnp.arange(steps_n)[:, None] >= jnp.arange(steps_n)[None, :]
    masked = jnp.where(causal, scores, very_low)
    highest = jnp.max(masked, axis=-1)
    weights = jnp.where(causal, jnp.exp(masked - highest[..., None]), 0.0)
    totals = jnp.sum(weights, axis=-1)
    summed = jnp.einsum(
        "bkgsu,ubkd->bkgsd",
        weights.astype(jnp.bfloat16),
        value_heads,
        preferred_element_type=jnp.float32,
    )
    return arrange(highest, totals, summed, steps_n * batch_size)


def local_small(
    hidden,
    norm_gain,
    w_query,
    w_key,
    w_value,
    w_output,
    key_cache,
    value_cache,
    retrieval,
    page_table,
    lengths,
    window_start,
):
    steps_n, batch_size, width_local = hidden.shape
    row_count = steps_n * batch_size
    page_count, page_len, kv_heads, head_dim = key_cache.shape
    query_width = w_query.shape[1]
    head_count = query_width // head_dim
    floated = hidden.astype(jnp.float32)
    squares = jnp.sum(floated * floated, axis=-1).reshape(row_count, 1)
    normed = (
        (floated * norm_gain.astype(jnp.float32))
        .astype(jnp.bfloat16)
        .reshape(row_count, width_local)
    )
    query_part = jnp.dot(normed, w_query, preferred_element_type=jnp.float32)
    key_part = jnp.dot(normed, w_key, preferred_element_type=jnp.float32)
    value_part = jnp.dot(normed, w_value, preferred_element_type=jnp.float32)
    query_sum, key_sum, value_sum, square_sum = lax.psum(
        (query_part, key_part, value_part, squares), "ctx"
    )
    inv_rms = lax.rsqrt(square_sum / D + epsilon)
    query_heads = (
        (query_sum * inv_rms)
        .astype(jnp.bfloat16)
        .reshape(steps_n, batch_size, kv_heads, head_count // kv_heads, head_dim)
    )
    key_heads = (
        (key_sum * inv_rms).astype(jnp.bfloat16).reshape(steps_n, batch_size, kv_heads, head_dim)
    )
    value_heads = (
        (value_sum * inv_rms).astype(jnp.bfloat16).reshape(steps_n, batch_size, kv_heads, head_dim)
    )
    device = lax.axis_index("ctx")
    local_parts = page_partials(
        query_heads,
        key_cache,
        value_cache,
        retrieval,
        page_table,
        lengths,
        window_start,
        device * page_count,
    )
    fresh_parts = fresh_partials(query_heads, key_heads, value_heads)
    col_share = query_width // lax.axis_size("ctx")
    col_start = device * col_share
    merged = merged_2(local_parts, "ctx", combine)
    highest, totals, summed = combine(merged, fresh_parts)
    attended_full = (
        (summed / totals[..., None]).reshape(row_count, query_width).astype(jnp.bfloat16)
    )
    attended = lax.dynamic_slice_in_dim(attended_full, col_start, col_share, 1)
    partial_out = jnp.dot(attended, w_output, preferred_element_type=jnp.float32)
    reduced = lax.psum_scatter(partial_out, "ctx", scatter_dimension=1, tiled=True)
    return reduced.reshape(steps_n, batch_size, -1).astype(jnp.bfloat16)


log2_e = 1.4426950408889634
chips = 8
far_away = 2**30


def fused(
    n,
    steps_n,
    batch,
    page_len,
    retrieval_hbm,
    lengths_hbm,
    window_hbm,
    hidden_hbm,
    gain_hbm,
    table_hbm,
    wq_hbm,
    wk_hbm,
    wv_hbm,
    wo_hbm,
    keys_hbm,
    values_hbm,
    out_ref,
    retrieval_ref,
    lengths_ref,
    window_ref,
    hidden_ref,
    gain_ref,
    table_ref,
    wq_v,
    wkv_v,
    wo_v,
    keys_v,
    values_v,
    keys_t,
    values_k,
    apart,
    bias,
    msg1,
    twin1,
    recv1,
    fresh_kv,
    gath,
    part3,
    twin3,
    msg3,
    recv3,
    out_own,
    out_other,
    twin4,
    recv4,
    load_sem,
    send_sem,
    recv_sem,
):
    f32, bf16 = jnp.float32, jnp.bfloat16
    me = lax.axis_index("ctx")
    chip, core = me // 2, lax.rem(me, 2)
    other = 1 - core
    pages = keys_v.shape[0]
    dim = 128
    rows = steps_n * batch
    heads_own = 4
    q_rows = heads_own * rows
    share = heads_own * dim
    width_local = hidden_ref.shape[2]
    scale = dim ** (-0.5) * log2_e

    def apart_by(a, b):
        where = 0
        for bit in (1, 2, 4):
            p, q = lax.rem(a // bit, 2), (b // bit) % 2
            where = where + bit * (p + q - 2 * p * q)
        return where

    def chip_at(i):
        return apart_by(chip, i)

    def peer(i, c=None):
        return 2 * chip_at(i) + (core if c is None else c)

    def in_turn(t):
        return apart_by(chip, lax.rem(chip + t, chips))

    far_in = 6

    twin = 2 * chip + other

    def load(k, from_ref, to_ref):
        return pltpu.make_async_copy(from_ref, to_ref, load_sem.at[k])

    sums_twin, sums_far, kv_twin, parts_far, outs_twin, outs_far = range(6)
    query_far, query_twin, parts_twin = range(6, 9)

    def remote(kind, i, from_ref, to_ref, device):
        return pltpu.make_async_remote_copy(
            src_ref=from_ref,
            dst_ref=to_ref,
            send_sem=send_sem.at[kind],
            recv_sem=recv_sem.at[kind if kind < 6 else 6 + chips * (kind - 6) + i],
            device_id={"ctx": device},
            device_id_type=pl.DeviceIdType.MESH,
        )

    kv_width = wk_hbm.shape[1]
    quarter = wq_hbm.shape[1] // 4
    load_kv = [
        load(0, wk_hbm, wkv_v.at[:, pl.ds(0, kv_width)]),
        load(0, wv_hbm, wkv_v.at[:, pl.ds(kv_width, kv_width)]),
    ]
    load_wo = load(1, wo_hbm, wo_v)
    load_keys = load(2, keys_hbm, keys_v)
    load_values = load(3, values_hbm, values_v)
    columns = [pl.ds(j * quarter, quarter) for j in range(4)]
    load_wq = [load(4 + j, wq_hbm.at[:, c], wq_v.at[:, c]) for j, c in enumerate(columns)]

    barrier = pltpu.get_barrier_semaphore()

    def greet(device):
        pl.semaphore_signal(
            barrier, inc=1, device_id={"ctx": device}, device_id_type=pl.DeviceIdType.MESH
        )

    @pl.loop(1, chips)
    def _(i):
        greet(peer(i))

    greet(twin)


    @pl.loop(far_in, chips)
    def _(i):
        greet(peer(i, other))

    load_small = [
        load(8 + j, from_ref, to_ref)
        for j, (from_ref, to_ref) in enumerate(
            (
                (hidden_hbm, hidden_ref),
                (gain_hbm, gain_ref),
                (table_hbm, table_ref),
                (lengths_hbm, lengths_ref),
                (window_hbm, window_ref),
                (retrieval_hbm, retrieval_ref),
            )
        )
    ]
    for copy in load_small + load_kv + load_wq:
        copy.start()
    for copy in load_small:
        copy.wait()

    loaded = hidden_ref[...].astype(f32)
    floated = jnp.concatenate(
        [loaded[s, b : b + 1, :] for b in range(batch) for s in range(steps_n)], axis=0
    )
    squares = jnp.sum(floated * floated, axis=1, keepdims=True)
    normed = (floated * gain_ref[...].astype(f32).reshape(1, width_local)).astype(bf16)

    sub = lax.broadcasted_iota(jnp.int32, (rows, dim), 0)
    lane = lax.broadcasted_iota(jnp.int32, (rows, dim), 1)
    squares = jnp.sum(jnp.where(lane == sub, squares, 0.0), axis=0, keepdims=True)
    first = sub < steps_n
    table = table_ref[...]
    page_id = lax.broadcasted_iota(jnp.int32, (pages, table.shape[1]), 0) + me * pages
    block = lax.broadcasted_iota(jnp.int32, (pages, table.shape[1]), 1).astype(f32)
    starts = []
    for b in range(batch):
        hit = jnp.where(table[b : b + 1, :] == page_id, 1.0, 0.0)
        found = jnp.sum(hit, axis=1, keepdims=True)
        start = jnp.sum(hit * block, axis=1, keepdims=True) * float(page_len)
        start = jnp.where(found > 0.0, start, float(far_away))
        starts.append(jnp.broadcast_to(start, (pages, dim)).astype(jnp.int32))
    until = jnp.where(first, lengths_ref[0], lengths_ref[1])
    since = jnp.where(first, window_ref[0], window_ref[1])
    for p in range(pages):
        position = jnp.where(first, starts[0][p : p + 1, :], starts[1][p : p + 1, :]) + lane
        cached = position < until
        recent = cached & ((position < SINKS) | (position >= since))
        bias[0, :, pl.ds(p * dim, dim)] = jnp.where(recent, 0.0, very_low)
        bias[1, :, pl.ds(p * dim, dim)] = jnp.where(cached, 0.0, very_low)

    load(0, wkv_v, wkv_v).wait()
    fresh = jnp.dot(normed, wkv_v[...], preferred_element_type=f32)
    for j in range(chips):
        slot = chip_at(j)
        for c in range(2):
            at = c * kv_width + j * dim
            msg1[c, slot, pl.ds(q_rows, rows), :] = fresh[:, at : at + dim]
            msg1[c, slot, pl.ds(q_rows + rows, 1), :] = squares
    for j in range(chips):
        if j % 2 == 0:
            load_wq[j // 2].wait()
        if j == 0:
            for copy in (load_keys, load_values, load_wo):
                copy.start()
        slot = chip_at(j)
        query = jnp.dot(
            normed, wq_v[:, pl.ds(j * 2 * share, 2 * share)], preferred_element_type=f32
        )
        for c in range(2):
            for g in range(heads_own):
                at = c * share + g * dim
                msg1[c, slot, pl.ds(g * rows, rows), :] = query[:, at : at + dim]

    pl.semaphore_wait(barrier, 2 * chips - far_in)

    joined1 = remote(sums_twin, 0, msg1.at[other], twin1, twin)
    joined1.start()
    joined1.wait_recv()

    @pl.loop(1, chips)
    def _(t):
        i = in_turn(t)
        msg1[core, i] = msg1[core, i] + twin1[i]
        remote(sums_far, 0, msg1.at[core, i], recv1.at[i], peer(i)).start()

    def by_head(p, slot, from_ref):
        apart[slot] = from_ref[p].astype(f32)
        return [apart[slot, pl.ds(k, page_len, stride=chips), :] for k in range(chips)]

    def turn_keys(p, slot):
        at = pl.ds(pl.multiple_of(p * page_len, page_len), page_len)
        for k, part in enumerate(by_head(p, slot, keys_v)):
            keys_t[k, :, at] = part.T.astype(bf16)

    def sort_values(p, slot):
        at = pl.ds(pl.multiple_of(p * page_len, page_len), page_len)
        for k, part in enumerate(by_head(p, slot, values_v)):
            values_k[k, at, :] = part.astype(bf16)

    load_keys.wait()

    @pl.loop(0, pages // 2)
    def _(h):
        for u in range(2):
            turn_keys(2 * h + u, u)

    load_values.wait()

    values_early = 3 * pages // 8

    @pl.loop(0, values_early)
    def _(h):
        for u in range(2):
            sort_values(2 * h + u, u)

    all_far = pl.ds(1, chips - 1)
    all1 = remote(sums_far, 0, msg1.at[core, all_far], recv1.at[all_far], twin)
    all1.wait_recv()
    summed = msg1[core, 0] + twin1[0]
    for i in range(1, chips):
        summed = summed + recv1[i]
    squares = jnp.where(lane == sub, summed[q_rows + rows :], 0.0)
    squares = jnp.sum(squares, axis=1, keepdims=True)
    inv_rms = lax.rsqrt(squares / (width_local * n) + epsilon)
    fresh_kv[core] = (summed[q_rows : q_rows + rows] * inv_rms).astype(bf16).astype(f32)
    for g in range(heads_own):
        piece = summed[g * rows : (g + 1) * rows] * inv_rms
        gath[0, core, pl.ds(g * rows, rows), :] = piece.astype(bf16).astype(f32)

    own = gath.at[0, core]

    def query_across(i, device):
        block = gath.at[i if i < far_in else 0, core]
        return remote(query_twin, i, block, gath.at[i, core], device)

    @pl.loop(1, chips)
    def _(t):
        i = in_turn(t)
        remote(query_far, i, own, gath.at[i, core], peer(i)).start()

    query_across(0, twin).start()
    kv_swap = remote(kv_twin, 0, fresh_kv.at[core], fresh_kv.at[core], twin)
    kv_swap.start()
    for i in range(far_in, chips):
        query_across(i, peer(i, other)).start()

    @pl.loop(values_early, pages // 2)
    def _(h):
        for u in range(2):
            sort_values(2 * h + u, u)

    def query_far_in(i):
        remote(query_far, i, own, gath.at[i, core], twin).wait_recv()

    def forward(i):
        query_far_in(i)
        query_across(i, twin).start()

    def arrived(i):
        if i >= far_in:
            query_far_in(i)
        block = gath.at[i, other]
        remote(query_twin, i, block, block, twin).wait_recv()

    def scores_of(i):
        k = chip_at(i)
        query = gath[i].reshape(2 * q_rows, dim).astype(bf16)
        scores = jnp.dot(query, keys_t[k], preferred_element_type=f32)
        hidden_by = bias[retrieval_ref[k]]
        scores = scores.reshape(2 * heads_own, rows, pages * page_len) * scale + hidden_by[None]
        return scores.reshape(2 * q_rows, pages * page_len)

    def fold(op, wide):
        parts = [wide[:, p * dim : (p + 1) * dim] for p in range(pages)]
        while len(parts) > 1:
            parts = [op(a, b) for a, b in zip(parts[::2], parts[1::2])]
        return parts[0]

    def weigh(scores):
        highest = jnp.max(fold(jnp.maximum, scores), axis=1, keepdims=True)
        weights = jnp.exp2(scores - highest)
        total = jnp.sum(fold(jnp.add, weights), axis=1, keepdims=True)
        return highest, total, weights.astype(bf16)

    def attend(offsets):
        scored = [scores_of(i) for i in offsets]
        weighed = [weigh(scores) for scores in scored]
        summed_up = [
            jnp.dot(weights, values_k[chip_at(i)], preferred_element_type=f32)
            for i, (_, _, weights) in zip(offsets, weighed)
        ]
        for i, summed, (highest, total, _) in zip(offsets, summed_up, weighed):
            highest = jnp.broadcast_to(highest, summed.shape)
            total = jnp.broadcast_to(total, summed.shape)
            for c in range(2):
                mine = slice(c * q_rows, (c + 1) * q_rows)
                part3[i, c, pl.ds(0, q_rows), :] = summed[mine]
                part3[i, c, pl.ds(q_rows, q_rows), :] = highest[mine]
                part3[i, c, pl.ds(2 * q_rows, q_rows), :] = total[mine]
        for i in offsets:
            part_swap(i).start()

    def part_swap(i):
        return remote(parts_twin, i, part3.at[i, other], twin3.at[i], twin)

    row = lax.broadcasted_iota(jnp.int32, (q_rows, dim), 0)
    col = lax.broadcasted_iota(jnp.int32, (q_rows, dim), 1)

    def stats_row(top, total):
        stats = jnp.where(col == row, top, 0.0) + jnp.where(col == row + q_rows, total, 0.0)
        return jnp.sum(stats, axis=0, keepdims=True)

    def join(i, to_ref):
        part_swap(i).wait_recv()
        a, b = part3[i, core], twin3[i]
        top_a, top_b = a[q_rows : 2 * q_rows], b[q_rows : 2 * q_rows]
        top = jnp.maximum(top_a, top_b)
        factor_a, factor_b = jnp.exp2(top_a - top), jnp.exp2(top_b - top)
        total = a[2 * q_rows :] * factor_a + b[2 * q_rows :] * factor_b
        to_ref[pl.ds(0, q_rows), :] = a[:q_rows] * factor_a + b[:q_rows] * factor_b
        to_ref[pl.ds(q_rows, 1), :] = stats_row(top, total)

    def pass_on(offsets):
        for i in offsets:
            join(i, msg3.at[i])
            remote(parts_far, 0, msg3.at[i], recv3.at[i], peer(i)).start()

    arrived(0)
    attend([0])
    for i in range(1, 4): forward(i)
    for i in (1,2,3): arrived(i)
    attend([1, 2, 3])
    for i in range(4, 6): forward(i)
    join(0, recv3.at[0])
    for i in (6,7): arrived(i)
    attend([6, 7])
    pass_on((1,2,3))
    for i in (4,5): arrived(i)
    attend([4, 5])
    pass_on((6,7))
    pass_on((4,5))
    remote(kv_twin, 0, fresh_kv.at[other], fresh_kv.at[other], twin).wait_recv()

    new_key = jnp.concatenate([fresh_kv[0]] * (dim // rows), axis=0).astype(bf16)
    new_value = jnp.concatenate([fresh_kv[1]] * (dim // rows), axis=0).astype(bf16)
    scores = lax.dot_general(
        gath[0, core].astype(bf16), new_key, (((1,), (1,)), ((), ())), preferred_element_type=f32
    )
    token = lax.rem(row, rows)
    causal = (col < rows) & (col // steps_n == token // steps_n) & (col <= token)
    scores = jnp.where(causal, scores * scale, very_low)
    fresh_top = jnp.max(scores, axis=1, keepdims=True)
    weights = jnp.where(causal, jnp.exp2(scores - fresh_top), 0.0)
    fresh_total = jnp.sum(weights, axis=1, keepdims=True)
    fresh_sum = jnp.dot(weights.astype(bf16), new_value, preferred_element_type=f32)

    load_wo.wait()

    all3 = remote(parts_far, 0, msg3.at[all_far], recv3.at[all_far], twin)
    all3.wait_recv()

    parts = [recv3.at[i] for i in range(chips)]
    count = len(parts)
    stats = jnp.zeros((rows, dim), f32)
    for k, part in enumerate(parts):
        stats = jnp.where(sub == k, part[pl.ds(q_rows, 1), :], stats)
    stats = jnp.concatenate([stats] * (dim // rows), axis=0).T
    top = jnp.where(col < count, stats[:q_rows], jnp.where(col == count, fresh_top, very_low))
    total = jnp.where(
        col < count, stats[q_rows : 2 * q_rows], jnp.where(col == count, fresh_total, 0.0)
    )
    factor = jnp.exp2(top - jnp.max(top, axis=1, keepdims=True))
    factor = factor / jnp.sum(factor * total, axis=1, keepdims=True)
    acc = fresh_sum * factor[:, count : count + 1]
    for k, part in enumerate(parts):
        acc += part[pl.ds(0, q_rows), :] * factor[:, k : k + 1]
    attended = jnp.concatenate(
        [acc[g * rows : (g + 1) * rows] for g in range(heads_own)], axis=1
    ).astype(bf16)

    def project_out(j, c):
        at = pl.multiple_of((2 * j + c) * share, share)
        return jnp.dot(attended, wo_v[:, pl.ds(at, share)], preferred_element_type=f32)

    for j in range(chips):
        out_other[chip_at(j)] = project_out(j, other)
    joined4 = remote(outs_twin, 0, out_other, twin4, twin)
    joined4.start()
    for j in range(chips):
        out_own[chip_at(j)] = project_out(j, core)
    joined4.wait_recv()

    @pl.loop(1, chips)
    def _(t):
        i = in_turn(t)
        out_own[i] = out_own[i] + twin4[i]
        remote(outs_far, 0, out_own.at[i], recv4.at[i], peer(i)).start()

    all4 = remote(outs_far, 0, out_own.at[all_far], recv4.at[all_far], twin)
    all4.wait_recv()
    result = out_own[0] + twin4[0]
    for i in range(1, chips):
        result = result + recv4[i]
    for s in range(steps_n):
        out_ref[s] = jnp.concatenate(
            [result[b * steps_n + s : b * steps_n + s + 1] for b in range(batch)], axis=0
        ).astype(out_ref.dtype)

    queries_out, queries_on = gath.at[all_far, core], gath.at[:, core]
    swapped = part3.at[:, other]
    for copy in (
        joined1,
        all1,
        remote(query_far, 0, queries_out, queries_out, twin),
        remote(query_twin, 0, queries_on, queries_on, twin),
        kv_swap,
        remote(parts_twin, 0, swapped, swapped, twin),
        all3,
        joined4,
        all4,
    ):
        copy.wait_send()


def local(
    hidden,
    norm_gain,
    w_query,
    w_key,
    w_value,
    w_output,
    key_cache,
    value_cache,
    retrieval,
    page_table,
    lengths,
    window_start,
):
    n = lax.axis_size("ctx")
    steps_n, batch, width_local = hidden.shape
    pages, page_len, kv_heads, dim = key_cache.shape
    query_width = w_query.shape[1]
    share = query_width // n
    rows = steps_n * batch
    q_rows = query_width // dim * steps_n
    if pages % 4 or (n, share, rows, batch, kv_heads, dim, page_len) != (16, 512, 8, 2, 8, 128, 128):
        return local_small(
            hidden,
            norm_gain,
            w_query,
            w_key,
            w_value,
            w_output,
            key_cache,
            value_cache,
            retrieval,
            page_table,
            lengths,
            window_start,
        )
    f32, bf16 = jnp.float32, jnp.bfloat16
    vmem = pl.BlockSpec(memory_space=pltpu.VMEM)
    hbm = pl.BlockSpec(memory_space=pl.ANY)
    dma = pltpu.SemaphoreType.DMA
    positions = pages * page_len
    out = pl.pallas_call(
        functools.partial(fused, n, steps_n, batch, page_len),
        out_shape=pltpu.VMEM((steps_n, batch, w_output.shape[1] // n), bf16),
        in_specs=[hbm] * 12,
        out_specs=vmem,
        scratch_shapes=[
            pltpu.SMEM(retrieval.shape, jnp.int32),
            pltpu.SMEM(lengths.shape, jnp.int32),
            pltpu.SMEM(window_start.shape, jnp.int32),
            pltpu.VMEM(hidden.shape, bf16),
            pltpu.VMEM(norm_gain.shape, bf16),
            pltpu.VMEM(page_table.shape, jnp.int32),
            pltpu.VMEM((width_local, query_width), bf16),
            pltpu.VMEM((width_local, 2 * kv_heads * dim), bf16),
            pltpu.VMEM((share, w_output.shape[1]), bf16),
            pltpu.VMEM((pages, page_len * kv_heads, dim), bf16),
            pltpu.VMEM((pages, page_len * kv_heads, dim), bf16),
            pltpu.VMEM((kv_heads, dim, positions), bf16),
            pltpu.VMEM((kv_heads, positions, dim), bf16),
            pltpu.VMEM((2, page_len * kv_heads, dim), f32),
            pltpu.VMEM((2, rows, positions), f32),
            pltpu.VMEM((2, chips, 41, dim), f32),
            pltpu.VMEM((chips, 41, dim), f32),
            pltpu.VMEM((chips, 41, dim), f32),
            pltpu.VMEM((2, rows, dim), f32),
            pltpu.VMEM((chips, 2, 32, dim), f32),
            pltpu.VMEM((chips, 2, 96, dim), f32),
            pltpu.VMEM((chips, 96, dim), f32),
            pltpu.VMEM((chips, 33, dim), f32),
            pltpu.VMEM((chips, 33, dim), f32),
            pltpu.VMEM((chips, rows, share), f32),
            pltpu.VMEM((chips, rows, share), f32),
            pltpu.VMEM((chips, rows, share), f32),
            pltpu.VMEM((chips, rows, share), f32),
            dma((14,)),
            dma((9,)),
            dma((6 + 3 * chips,)),
        ],
        compiler_params=pltpu.CompilerParams(
            collective_id=0, has_side_effects=True, vmem_limit_bytes=56 * 2**20
        ),
    )(
        retrieval,
        lengths,
        window_start,
        hidden,
        norm_gain,
        page_table,
        w_query,
        w_key,
        w_value,
        w_output,
        key_cache.reshape(pages, page_len * kv_heads, dim),
        value_cache.reshape(pages, page_len * kv_heads, dim),
    )
    return out


def solution(mesh):
    placed = (
        P(None, "groups", "ctx"),
        P("ctx"),
        P("ctx", None),
        P("ctx", None),
        P("ctx", None),
        P("ctx", None),
        P(("groups", "ctx"), None, None, None),
        P(("groups", "ctx"), None, None, None),
        P(),
        P("groups", None),
        P("groups"),
        P("groups"),
    )
    return jax.shard_map(
        local, mesh=mesh, in_specs=placed, out_specs=P(None, "groups", "ctx"), check_vma=False
    )
```

```python
import functools

import jax
import jax.numpy as jnp
from jax import lax
from jax.experimental import pallas as pl
from jax.experimental.pallas import tpu as pltpu
from jax.sharding import PartitionSpec as P

D = 8192
SINKS = 4


very_low = -1e30
epsilon = 1e-05


def merged_2(shard, axis, combine):
    everything = jax.tree.map(lambda part: lax.all_gather(part, axis), shard)
    first = jax.tree.map(lambda part: part[0], everything)

    def turn(k, so_far):
        return combine(so_far, jax.tree.map(lambda part: part[k], everything))

    return lax.fori_loop(1, lax.axis_size(axis), turn, first)


def combine(earlier, later):
    top_a, total_a, summed_a = earlier
    top_b, total_b, summed_b = later
    highest = jnp.maximum(top_a, top_b)
    factor_a = jnp.exp(top_a - highest)
    factor_b = jnp.exp(top_b - highest)
    return (
        highest,
        total_a * factor_a + total_b * factor_b,
        summed_a * factor_a[..., None] + summed_b * factor_b[..., None],
    )


def arrange(top_val, total_val, summed_val, row_count):
    head_count = top_val.shape[1] * top_val.shape[2]
    top_val = jnp.transpose(top_val, (3, 0, 1, 2)).reshape(row_count, head_count)
    total_val = jnp.transpose(total_val, (3, 0, 1, 2)).reshape(row_count, head_count)
    summed_val = jnp.transpose(summed_val, (3, 0, 1, 2, 4)).reshape(
        row_count, head_count, summed_val.shape[-1]
    )
    return (top_val, total_val, summed_val)


def of_owner(values, owner_req, axis):
    picked = None
    for b in range(values.shape[axis]):
        entry = lax.slice_in_dim(values, b, b + 1, axis=axis)
        mine = (owner_req == b).reshape((-1,) + (1,) * (values.ndim - 1 - axis))
        picked = entry if picked is None else jnp.where(mine, entry, picked)
    shape = list(values.shape)
    shape[axis] = owner_req.shape[0]
    return jnp.broadcast_to(picked, shape)


def page_partials(
    query_heads, page_keys, page_values, retrieval, page_table, lengths, window_start, first_page
):
    page_count, page_len, kv_heads, head_dim = page_keys.shape
    batch_size, blocks = page_table.shape
    steps_n = query_heads.shape[0]
    slot_ids = first_page + jnp.arange(page_count, dtype=jnp.int32)
    matches = (page_table[None, :, :] == slot_ids[:, None, None]).astype(jnp.int32)
    owner_req = jnp.sum(
        matches * jnp.arange(batch_size, dtype=jnp.int32)[None, :, None], axis=(1, 2)
    )
    block_ids = jnp.sum(matches * jnp.arange(blocks, dtype=jnp.int32)[None, None, :], axis=(1, 2))
    query_page = of_owner(query_heads, owner_req, 1)
    scores = jnp.einsum(
        "spkgd,ptkd->pkgst", query_page, page_keys, preferred_element_type=jnp.float32
    ) * head_dim ** (-0.5)
    positions = block_ids[:, None] * page_len + jnp.arange(page_len, dtype=jnp.int32)[None, :]
    in_range = positions < of_owner(lengths, owner_req, 0)[:, None]
    recent = (positions < SINKS) | (positions >= of_owner(window_start, owner_req, 0)[:, None])
    visible = in_range[:, None, :] & ((retrieval[None, :, None] == 1) | recent[:, None, :])
    visible = visible[:, :, None, None, :]
    masked = jnp.where(visible, scores, very_low)
    owner_hot = owner_req[:, None] == jnp.arange(batch_size, dtype=jnp.int32)[None, :]
    page_max = jnp.max(masked, axis=-1)
    local_max = jnp.max(
        jnp.where(owner_hot[:, :, None, None, None], page_max[:, None], very_low), axis=0
    )
    row_max = of_owner(local_max, owner_req, 0)
    weights = jnp.where(visible, jnp.exp(masked - row_max[..., None]), 0.0)
    owner_float = owner_hot.astype(jnp.float32)
    local_total = jnp.einsum(
        "pb,pkgs->bkgs", owner_float, jnp.sum(weights, axis=-1), precision=lax.Precision.HIGHEST
    )
    values = jnp.einsum(
        "pkgst,ptkd->pkgsd",
        weights.astype(jnp.bfloat16),
        page_values,
        preferred_element_type=jnp.float32,
    )
    local_sum = jnp.einsum("pb,pkgsd->bkgsd", owner_float, values, precision=lax.Precision.HIGHEST)
    return arrange(local_max, local_total, local_sum, steps_n * batch_size)


def fresh_partials(query_heads, key_heads, value_heads):
    steps_n, batch_size, kv_heads, group, head_dim = query_heads.shape
    scores = jnp.einsum(
        "sbkgd,ubkd->bkgsu", query_heads, key_heads, preferred_element_type=jnp.float32
    ) * head_dim ** (-0.5)
    causal = jnp.arange(steps_n)[:, None] >= jnp.arange(steps_n)[None, :]
    masked = jnp.where(causal, scores, very_low)
    highest = jnp.max(masked, axis=-1)
    weights = jnp.where(causal, jnp.exp(masked - highest[..., None]), 0.0)
    totals = jnp.sum(weights, axis=-1)
    summed = jnp.einsum(
        "bkgsu,ubkd->bkgsd",
        weights.astype(jnp.bfloat16),
        value_heads,
        preferred_element_type=jnp.float32,
    )
    return arrange(highest, totals, summed, steps_n * batch_size)


def local_small(
    hidden,
    norm_gain,
    w_query,
    w_key,
    w_value,
    w_output,
    key_cache,
    value_cache,
    retrieval,
    page_table,
    lengths,
    window_start,
):
    steps_n, batch_size, width_local = hidden.shape
    row_count = steps_n * batch_size
    page_count, page_len, kv_heads, head_dim = key_cache.shape
    query_width = w_query.shape[1]
    head_count = query_width // head_dim
    floated = hidden.astype(jnp.float32)
    squares = jnp.sum(floated * floated, axis=-1).reshape(row_count, 1)
    normed = (
        (floated * norm_gain.astype(jnp.float32))
        .astype(jnp.bfloat16)
        .reshape(row_count, width_local)
    )
    query_part = jnp.dot(normed, w_query, preferred_element_type=jnp.float32)
    key_part = jnp.dot(normed, w_key, preferred_element_type=jnp.float32)
    value_part = jnp.dot(normed, w_value, preferred_element_type=jnp.float32)
    query_sum, key_sum, value_sum, square_sum = lax.psum(
        (query_part, key_part, value_part, squares), "ctx"
    )
    inv_rms = lax.rsqrt(square_sum / D + epsilon)
    query_heads = (
        (query_sum * inv_rms)
        .astype(jnp.bfloat16)
        .reshape(steps_n, batch_size, kv_heads, head_count // kv_heads, head_dim)
    )
    key_heads = (
        (key_sum * inv_rms).astype(jnp.bfloat16).reshape(steps_n, batch_size, kv_heads, head_dim)
    )
    value_heads = (
        (value_sum * inv_rms).astype(jnp.bfloat16).reshape(steps_n, batch_size, kv_heads, head_dim)
    )
    device = lax.axis_index("ctx")
    local_parts = page_partials(
        query_heads,
        key_cache,
        value_cache,
        retrieval,
        page_table,
        lengths,
        window_start,
        device * page_count,
    )
    fresh_parts = fresh_partials(query_heads, key_heads, value_heads)
    col_share = query_width // lax.axis_size("ctx")
    col_start = device * col_share
    merged = merged_2(local_parts, "ctx", combine)
    highest, totals, summed = combine(merged, fresh_parts)
    attended_full = (
        (summed / totals[..., None]).reshape(row_count, query_width).astype(jnp.bfloat16)
    )
    attended = lax.dynamic_slice_in_dim(attended_full, col_start, col_share, 1)
    partial_out = jnp.dot(attended, w_output, preferred_element_type=jnp.float32)
    reduced = lax.psum_scatter(partial_out, "ctx", scatter_dimension=1, tiled=True)
    return reduced.reshape(steps_n, batch_size, -1).astype(jnp.bfloat16)


log2_e = 1.4426950408889634
chips = 8
far_away = 2**30


def fused(
    n,
    steps_n,
    batch,
    page_len,
    retrieval_hbm,
    lengths_hbm,
    window_hbm,
    hidden_hbm,
    gain_hbm,
    table_hbm,
    wq_hbm,
    wk_hbm,
    wv_hbm,
    wo_hbm,
    keys_hbm,
    values_hbm,
    out_ref,
    retrieval_ref,
    lengths_ref,
    window_ref,
    hidden_ref,
    gain_ref,
    table_ref,
    wq_v,
    wkv_v,
    wo_v,
    keys_v,
    values_v,
    keys_t,
    values_k,
    apart,
    bias,
    msg1,
    twin1,
    recv1,
    fresh_kv,
    gath,
    part3,
    twin3,
    msg3,
    recv3,
    out_own,
    out_other,
    twin4,
    recv4,
    load_sem,
    send_sem,
    recv_sem,
):
    f32, bf16 = jnp.float32, jnp.bfloat16
    me = lax.axis_index("ctx")
    chip, core = me // 2, lax.rem(me, 2)
    other = 1 - core
    pages = keys_v.shape[0]
    dim = 128
    rows = steps_n * batch
    heads_own = 4
    q_rows = heads_own * rows
    share = heads_own * dim
    width_local = hidden_ref.shape[2]
    scale = dim ** (-0.5) * log2_e

    def apart_by(a, b):
        where = 0
        for bit in (1, 2, 4):
            p, q = lax.rem(a // bit, 2), (b // bit) % 2
            where = where + bit * (p + q - 2 * p * q)
        return where

    def chip_at(i):
        return apart_by(chip, i)

    def peer(i, c=None):
        return 2 * chip_at(i) + (core if c is None else c)

    def next_device(t):
        return 2 * lax.rem(chip + t, chips) + core

    def steps_to(j):
        return lax.rem(j + chips - chip, chips)

    def in_turn(t):
        return apart_by(chip, lax.rem(chip + t, chips))

    far_in = 6

    twin = 2 * chip + other

    def load(k, from_ref, to_ref):
        return pltpu.make_async_copy(from_ref, to_ref, load_sem.at[k])

    sums_twin, sums_far, kv_twin, parts_far, outs_twin, outs_far = range(6)
    query_far, query_twin, parts_twin = range(6, 9)

    def remote(kind, i, from_ref, to_ref, device):
        return pltpu.make_async_remote_copy(
            src_ref=from_ref,
            dst_ref=to_ref,
            send_sem=send_sem.at[kind],
            recv_sem=recv_sem.at[kind if kind < 6 else 6 + chips * (kind - 6) + i],
            device_id={"ctx": device},
            device_id_type=pl.DeviceIdType.MESH,
        )

    kv_width = wk_hbm.shape[1]
    quarter = wq_hbm.shape[1] // 4
    load_kv = [
        load(0, wk_hbm, wkv_v.at[:, pl.ds(0, kv_width)]),
        load(0, wv_hbm, wkv_v.at[:, pl.ds(kv_width, kv_width)]),
    ]
    load_wo = load(1, wo_hbm, wo_v)
    load_keys = load(2, keys_hbm, keys_v)
    load_values = load(3, values_hbm, values_v)
    columns = [pl.ds(j * quarter, quarter) for j in range(4)]
    load_wq = [load(4 + j, wq_hbm.at[:, c], wq_v.at[:, c]) for j, c in enumerate(columns)]

    barrier = pltpu.get_barrier_semaphore()

    def greet(device):
        pl.semaphore_signal(
            barrier, inc=1, device_id={"ctx": device}, device_id_type=pl.DeviceIdType.MESH
        )

    @pl.loop(1, chips)
    def _(i):
        greet(peer(i))

    greet(twin)


    @pl.loop(far_in, chips)
    def _(i):
        greet(peer(i, other))

    load_small = [
        load(8 + j, from_ref, to_ref)
        for j, (from_ref, to_ref) in enumerate(
            (
                (hidden_hbm, hidden_ref),
                (gain_hbm, gain_ref),
                (table_hbm, table_ref),
                (lengths_hbm, lengths_ref),
                (window_hbm, window_ref),
                (retrieval_hbm, retrieval_ref),
            )
        )
    ]
    for copy in load_small + load_kv + load_wq:
        copy.start()
    for copy in load_small:
        copy.wait()

    loaded = hidden_ref[...].astype(f32)
    floated = jnp.concatenate(
        [loaded[s, b : b + 1, :] for b in range(batch) for s in range(steps_n)], axis=0
    )
    squares = jnp.sum(floated * floated, axis=1, keepdims=True)
    normed = (floated * gain_ref[...].astype(f32).reshape(1, width_local)).astype(bf16)

    sub = lax.broadcasted_iota(jnp.int32, (rows, dim), 0)
    lane = lax.broadcasted_iota(jnp.int32, (rows, dim), 1)
    squares = jnp.sum(jnp.where(lane == sub, squares, 0.0), axis=0, keepdims=True)
    first = sub < steps_n
    table = table_ref[...]
    page_id = lax.broadcasted_iota(jnp.int32, (pages, table.shape[1]), 0) + me * pages
    block = lax.broadcasted_iota(jnp.int32, (pages, table.shape[1]), 1).astype(f32)
    starts = []
    for b in range(batch):
        hit = jnp.where(table[b : b + 1, :] == page_id, 1.0, 0.0)
        found = jnp.sum(hit, axis=1, keepdims=True)
        start = jnp.sum(hit * block, axis=1, keepdims=True) * float(page_len)
        start = jnp.where(found > 0.0, start, float(far_away))
        starts.append(jnp.broadcast_to(start, (pages, dim)).astype(jnp.int32))
    until = jnp.where(first, lengths_ref[0], lengths_ref[1])
    since = jnp.where(first, window_ref[0], window_ref[1])
    for p in range(pages):
        position = jnp.where(first, starts[0][p : p + 1, :], starts[1][p : p + 1, :]) + lane
        cached = position < until
        recent = cached & ((position < SINKS) | (position >= since))
        bias[0, :, pl.ds(p * dim, dim)] = jnp.where(recent, 0.0, very_low)
        bias[1, :, pl.ds(p * dim, dim)] = jnp.where(cached, 0.0, very_low)

    load(0, wkv_v, wkv_v).wait()
    fresh = jnp.dot(normed, wkv_v[...], preferred_element_type=f32)
    for j in range(chips):
        slot = steps_to(j)
        for c in range(2):
            at = c * kv_width + j * dim
            msg1[c, slot, pl.ds(q_rows, rows), :] = fresh[:, at : at + dim]
            msg1[c, slot, pl.ds(q_rows + rows, 1), :] = squares
    for j in range(chips):
        if j % 2 == 0:
            load_wq[j // 2].wait()
        if j == 0:
            for copy in (load_keys, load_values):
                copy.start()
        slot = steps_to(j)
        query = jnp.dot(
            normed, wq_v[:, pl.ds(j * 2 * share, 2 * share)], preferred_element_type=f32
        )
        for c in range(2):
            for g in range(heads_own):
                at = c * share + g * dim
                msg1[c, slot, pl.ds(g * rows, rows), :] = query[:, at : at + dim]

    pl.semaphore_wait(barrier, 2 * chips - far_in)

    joined1 = remote(sums_twin, 0, msg1.at[other], twin1, twin)
    joined1.start()
    joined1.wait_recv()

    @pl.loop(1, chips)
    def _(t):
        msg1[core, t] = msg1[core, t] + twin1[t]
        remote(sums_far, 0, msg1.at[core, t], recv1.at[t], next_device(t)).start()

    def by_head(p, slot, from_ref):
        apart[slot] = from_ref[p].astype(f32)
        return [apart[slot, pl.ds(k, page_len, stride=chips), :] for k in range(chips)]

    def turn_keys(p, slot):
        at = pl.ds(pl.multiple_of(p * page_len, page_len), page_len)
        for k, part in enumerate(by_head(p, slot, keys_v)):
            keys_t[k, :, at] = part.T.astype(bf16)

    def sort_values(p, slot):
        at = pl.ds(pl.multiple_of(p * page_len, page_len), page_len)
        for k, part in enumerate(by_head(p, slot, values_v)):
            values_k[k, at, :] = part.astype(bf16)

    load_keys.wait()

    @pl.loop(0, pages // 2)
    def _(h):
        for u in range(2):
            turn_keys(2 * h + u, u)

    load_values.wait()

    values_early = 3 * pages // 8

    @pl.loop(0, values_early)
    def _(h):
        for u in range(2):
            sort_values(2 * h + u, u)

    all_far = pl.ds(1, chips - 1)
    all1 = remote(sums_far, 0, msg1.at[core, all_far], recv1.at[all_far], twin)
    all1.wait_recv()
    summed = msg1[core, 0] + twin1[0]
    for i in range(1, chips):
        summed = summed + recv1[i]
    squares = jnp.where(lane == sub, summed[q_rows + rows :], 0.0)
    squares = jnp.sum(squares, axis=1, keepdims=True)
    inv_rms = lax.rsqrt(squares / (width_local * n) + epsilon)
    fresh_kv[core] = (summed[q_rows : q_rows + rows] * inv_rms).astype(bf16).astype(f32)
    for g in range(heads_own):
        piece = summed[g * rows : (g + 1) * rows] * inv_rms
        gath[0, core, pl.ds(g * rows, rows), :] = piece.astype(bf16).astype(f32)

    own = gath.at[0, core]

    def query_across(i, device):
        block = gath.at[i if i < far_in else 0, core]
        return remote(query_twin, i, block, gath.at[i, core], device)

    @pl.loop(1, chips)
    def _(t):
        i = in_turn(t)
        remote(query_far, i, own, gath.at[i, core], next_device(t)).start()

    query_across(0, twin).start()
    kv_swap = remote(kv_twin, 0, fresh_kv.at[core], fresh_kv.at[core], twin)
    kv_swap.start()
    for i in range(far_in, chips):
        query_across(i, peer(i, other)).start()

    load_wo.start()

    @pl.loop(values_early, pages // 2)
    def _(h):
        for u in range(2):
            sort_values(2 * h + u, u)

    def query_far_in(i):
        remote(query_far, i, own, gath.at[i, core], twin).wait_recv()

    def forward(i):
        query_far_in(i)
        query_across(i, twin).start()

    def arrived(i):
        if i >= far_in:
            query_far_in(i)
        block = gath.at[i, other]
        remote(query_twin, i, block, block, twin).wait_recv()

    def scores_of(i):
        k = chip_at(i)
        query = gath[i].reshape(2 * q_rows, dim).astype(bf16)
        scores = jnp.dot(query, keys_t[k], preferred_element_type=f32)
        hidden_by = bias[retrieval_ref[k]]
        scores = scores.reshape(2 * heads_own, rows, pages * page_len) * scale + hidden_by[None]
        return scores.reshape(2 * q_rows, pages * page_len)

    def fold(op, wide):
        parts = [wide[:, p * dim : (p + 1) * dim] for p in range(pages)]
        while len(parts) > 1:
            parts = [op(a, b) for a, b in zip(parts[::2], parts[1::2])]
        return parts[0]

    def weigh(scores):
        highest = jnp.max(fold(jnp.maximum, scores), axis=1, keepdims=True)
        weights = jnp.exp2(scores - highest)
        total = jnp.sum(fold(jnp.add, weights), axis=1, keepdims=True)
        return highest, total, weights.astype(bf16)

    def attend(offsets):
        scored = [scores_of(i) for i in offsets]
        weighed = [weigh(scores) for scores in scored]
        summed_up = [
            jnp.dot(weights, values_k[chip_at(i)], preferred_element_type=f32)
            for i, (_, _, weights) in zip(offsets, weighed)
        ]
        for i, summed, (highest, total, _) in zip(offsets, summed_up, weighed):
            highest = jnp.broadcast_to(highest, summed.shape)
            total = jnp.broadcast_to(total, summed.shape)
            for c in range(2):
                mine = slice(c * q_rows, (c + 1) * q_rows)
                part3[i, c, pl.ds(0, q_rows), :] = summed[mine]
                part3[i, c, pl.ds(q_rows, q_rows), :] = highest[mine]
                part3[i, c, pl.ds(2 * q_rows, q_rows), :] = total[mine]
        for i in offsets:
            part_swap(i).start()

    def part_swap(i):
        return remote(parts_twin, i, part3.at[i, other], twin3.at[i], twin)

    row = lax.broadcasted_iota(jnp.int32, (q_rows, dim), 0)
    col = lax.broadcasted_iota(jnp.int32, (q_rows, dim), 1)

    def stats_row(top, total):
        stats = jnp.where(col == row, top, 0.0) + jnp.where(col == row + q_rows, total, 0.0)
        return jnp.sum(stats, axis=0, keepdims=True)

    def join(i, to_ref):
        part_swap(i).wait_recv()
        a, b = part3[i, core], twin3[i]
        top_a, top_b = a[q_rows : 2 * q_rows], b[q_rows : 2 * q_rows]
        top = jnp.maximum(top_a, top_b)
        factor_a, factor_b = jnp.exp2(top_a - top), jnp.exp2(top_b - top)
        total = a[2 * q_rows :] * factor_a + b[2 * q_rows :] * factor_b
        to_ref[pl.ds(0, q_rows), :] = a[:q_rows] * factor_a + b[:q_rows] * factor_b
        to_ref[pl.ds(q_rows, 1), :] = stats_row(top, total)

    def pass_on(offsets):
        for i in offsets:
            join(i, msg3.at[i])
            remote(parts_far, 0, msg3.at[i], recv3.at[i], peer(i)).start()

    arrived(0)
    attend([0])
    for i in range(1, 4): forward(i)
    for i in (1,2,3): arrived(i)
    attend([1, 2, 3])
    for i in range(4, 6): forward(i)
    join(0, recv3.at[0])
    for i in (6,7): arrived(i)
    attend([6, 7])
    pass_on((1,2,3))
    for i in (4,5): arrived(i)
    attend([4, 5])
    pass_on((6,7))
    pass_on((4,5))
    remote(kv_twin, 0, fresh_kv.at[other], fresh_kv.at[other], twin).wait_recv()

    new_key = jnp.concatenate([fresh_kv[0]] * (dim // rows), axis=0).astype(bf16)
    new_value = jnp.concatenate([fresh_kv[1]] * (dim // rows), axis=0).astype(bf16)
    scores = lax.dot_general(
        gath[0, core].astype(bf16), new_key, (((1,), (1,)), ((), ())), preferred_element_type=f32
    )
    token = lax.rem(row, rows)
    causal = (col < rows) & (col // steps_n == token // steps_n) & (col <= token)
    scores = jnp.where(causal, scores * scale, very_low)
    fresh_top = jnp.max(scores, axis=1, keepdims=True)
    weights = jnp.where(causal, jnp.exp2(scores - fresh_top), 0.0)
    fresh_total = jnp.sum(weights, axis=1, keepdims=True)
    fresh_sum = jnp.dot(weights.astype(bf16), new_value, preferred_element_type=f32)

    load_wo.wait()

    all3 = remote(parts_far, 0, msg3.at[all_far], recv3.at[all_far], twin)
    all3.wait_recv()

    parts = [recv3.at[i] for i in range(chips)]
    count = len(parts)
    stats = jnp.zeros((rows, dim), f32)
    for k, part in enumerate(parts):
        stats = jnp.where(sub == k, part[pl.ds(q_rows, 1), :], stats)
    stats = jnp.concatenate([stats] * (dim // rows), axis=0).T
    top = jnp.where(col < count, stats[:q_rows], jnp.where(col == count, fresh_top, very_low))
    total = jnp.where(
        col < count, stats[q_rows : 2 * q_rows], jnp.where(col == count, fresh_total, 0.0)
    )
    factor = jnp.exp2(top - jnp.max(top, axis=1, keepdims=True))
    factor = factor / jnp.sum(factor * total, axis=1, keepdims=True)
    acc = fresh_sum * factor[:, count : count + 1]
    for k, part in enumerate(parts):
        acc += part[pl.ds(0, q_rows), :] * factor[:, k : k + 1]
    attended = jnp.concatenate(
        [acc[g * rows : (g + 1) * rows] for g in range(heads_own)], axis=1
    ).astype(bf16)

    def project_out(j, c):
        at = pl.multiple_of((2 * j + c) * share, share)
        return jnp.dot(attended, wo_v[:, pl.ds(at, share)], preferred_element_type=f32)

    for j in range(chips):
        out_other[steps_to(j)] = project_out(j, other)
    joined4 = remote(outs_twin, 0, out_other, twin4, twin)
    joined4.start()
    for j in range(chips):
        out_own[steps_to(j)] = project_out(j, core)
    joined4.wait_recv()

    @pl.loop(1, chips)
    def _(t):
        out_own[t] = out_own[t] + twin4[t]
        remote(outs_far, 0, out_own.at[t], recv4.at[t], next_device(t)).start()

    all4 = remote(outs_far, 0, out_own.at[all_far], recv4.at[all_far], twin)
    all4.wait_recv()
    result = out_own[0] + twin4[0]
    for i in range(1, chips):
        result = result + recv4[i]
    for s in range(steps_n):
        out_ref[s] = jnp.concatenate(
            [result[b * steps_n + s : b * steps_n + s + 1] for b in range(batch)], axis=0
        ).astype(out_ref.dtype)

    queries_out, queries_on = gath.at[all_far, core], gath.at[:, core]
    swapped = part3.at[:, other]
    for copy in (
        joined1,
        all1,
        remote(query_far, 0, queries_out, queries_out, twin),
        remote(query_twin, 0, queries_on, queries_on, twin),
        kv_swap,
        remote(parts_twin, 0, swapped, swapped, twin),
        all3,
        joined4,
        all4,
    ):
        copy.wait_send()


def local(
    hidden,
    norm_gain,
    w_query,
    w_key,
    w_value,
    w_output,
    key_cache,
    value_cache,
    retrieval,
    page_table,
    lengths,
    window_start,
):
    n = lax.axis_size("ctx")
    steps_n, batch, width_local = hidden.shape
    pages, page_len, kv_heads, dim = key_cache.shape
    query_width = w_query.shape[1]
    share = query_width // n
    rows = steps_n * batch
    q_rows = query_width // dim * steps_n
    if pages % 4 or (n, share, rows, batch, kv_heads, dim, page_len) != (16, 512, 8, 2, 8, 128, 128):
        return local_small(
            hidden,
            norm_gain,
            w_query,
            w_key,
            w_value,
            w_output,
            key_cache,
            value_cache,
            retrieval,
            page_table,
            lengths,
            window_start,
        )
    f32, bf16 = jnp.float32, jnp.bfloat16
    vmem = pl.BlockSpec(memory_space=pltpu.VMEM)
    hbm = pl.BlockSpec(memory_space=pl.ANY)
    dma = pltpu.SemaphoreType.DMA
    positions = pages * page_len
    out = pl.pallas_call(
        functools.partial(fused, n, steps_n, batch, page_len),
        out_shape=pltpu.VMEM((steps_n, batch, w_output.shape[1] // n), bf16),
        in_specs=[hbm] * 12,
        out_specs=vmem,
        scratch_shapes=[
            pltpu.SMEM(retrieval.shape, jnp.int32),
            pltpu.SMEM(lengths.shape, jnp.int32),
            pltpu.SMEM(window_start.shape, jnp.int32),
            pltpu.VMEM(hidden.shape, bf16),
            pltpu.VMEM(norm_gain.shape, bf16),
            pltpu.VMEM(page_table.shape, jnp.int32),
            pltpu.VMEM((width_local, query_width), bf16),
            pltpu.VMEM((width_local, 2 * kv_heads * dim), bf16),
            pltpu.VMEM((share, w_output.shape[1]), bf16),
            pltpu.VMEM((pages, page_len * kv_heads, dim), bf16),
            pltpu.VMEM((pages, page_len * kv_heads, dim), bf16),
            pltpu.VMEM((kv_heads, dim, positions), bf16),
            pltpu.VMEM((kv_heads, positions, dim), bf16),
            pltpu.VMEM((2, page_len * kv_heads, dim), f32),
            pltpu.VMEM((2, rows, positions), f32),
            pltpu.VMEM((2, chips, 41, dim), f32),
            pltpu.VMEM((chips, 41, dim), f32),
            pltpu.VMEM((chips, 41, dim), f32),
            pltpu.VMEM((2, rows, dim), f32),
            pltpu.VMEM((chips, 2, 32, dim), f32),
            pltpu.VMEM((chips, 2, 96, dim), f32),
            pltpu.VMEM((chips, 96, dim), f32),
            pltpu.VMEM((chips, 33, dim), f32),
            pltpu.VMEM((chips, 33, dim), f32),
            pltpu.VMEM((chips, rows, share), f32),
            pltpu.VMEM((chips, rows, share), f32),
            pltpu.VMEM((chips, rows, share), f32),
            pltpu.VMEM((chips, rows, share), f32),
            dma((14,)),
            dma((9,)),
            dma((6 + 3 * chips,)),
        ],
        compiler_params=pltpu.CompilerParams(
            collective_id=0, has_side_effects=True, vmem_limit_bytes=56 * 2**20
        ),
    )(
        retrieval,
        lengths,
        window_start,
        hidden,
        norm_gain,
        page_table,
        w_query,
        w_key,
        w_value,
        w_output,
        key_cache.reshape(pages, page_len * kv_heads, dim),
        value_cache.reshape(pages, page_len * kv_heads, dim),
    )
    return out


def solution(mesh):
    placed = (
        P(None, "groups", "ctx"),
        P("ctx"),
        P("ctx", None),
        P("ctx", None),
        P("ctx", None),
        P("ctx", None),
        P(("groups", "ctx"), None, None, None),
        P(("groups", "ctx"), None, None, None),
        P(),
        P("groups", None),
        P("groups"),
        P("groups"),
    )
    return jax.shard_map(
        local, mesh=mesh, in_specs=placed, out_specs=P(None, "groups", "ctx"), check_vma=False
    )
```
